128 devices in a mesh: dp: 32 (over x, z, y_hi), mp: 4 (over y_lo, core).
Axes of the slice: x: 4, y: 4 (y_hi: 2, y_lo: 2; y = y_hi * 2 + y_lo), z: 4, core: 2. Of those that a mesh axis runs over, the one named last changes fastest.
Arguments:
- activations: bfloat16 [32768, 8192], P('dp', 'mp'), may hold values from -6 to 6
- cot_true: bfloat16 [32768, 1024], P('dp', 'mp'), may hold values from -6 to 6
- cot_sampled: bfloat16 [32768, 1024], P('dp', 'mp'), may hold values from -6 to 6
- tile_mask: int32 [64, 8], replicated, may hold values from 0 to 1, as said below
- moment: float32 [8192, 1024], P('dp', 'mp'), may hold values from -0.0012207031 to 0.0012207031
- curvature: float32 [8192, 1024], P('dp', 'mp'), may hold values from 0.003 to 3
Outputs:
- update: float32 [8192, 1024], P('dp', 'mp')
- new_curvature: float32 [8192, 1024], P('dp', 'mp')
The draws below stay inside these ranges and needn't reach their ends.
Inputs may be any that keep to these rules, and one draw needn't show every extreme that they name: Every column of tile_mask holds exactly 16 ones.
All inputs are finite; a program needn't handle non-finite values.
Results may differ from the reference program's by a relative error of at most 0.0003.
Values may be sent and summed in bfloat16 or wider, within the bound.
A program may use at most 128 MiB of HBM per device.

```python
import math
import jax
import jax.numpy as jnp
from jax import lax

D = 8192
KVW = 1024
BLOCK = 128
TOKENS = 32768


def draw_tile_mask(key, part):
    tile_rows = D // BLOCK
    tile_cols = KVW // BLOCK
    column_keys = jax.random.split(key, tile_cols)
    orders = jax.vmap(lambda single: jax.random.permutation(single, tile_rows))(column_keys)
    return (orders < tile_rows // 4).astype(jnp.int32).T


def steps_of(own_key, dims, shards, least, high):
    def one(dim, blocks):
        steps = jax.random.uniform(jax.random.fold_in(jax.random.fold_in(own_key, 6), dim), (blocks,), jnp.float32, least / len(shards), high / len(shards))
        return jnp.repeat(jnp.exp(steps), dims[dim] // blocks).reshape((-1,) + (1,) * (len(dims) - dim - 1))

    level = one(*shards[0])
    for cut in shards[1:]:
        level = level * one(*cut)
    return level


def gaussian(rng, shape, deviation, reach, cuts=(), dtype=jnp.bfloat16):
    factor_of = steps_of(rng, shape, cuts, -0.22, 0.18) if cuts else 1.0
    entries = jax.random.normal(rng, shape, jnp.float32) * deviation * factor_of
    return jnp.minimum(jnp.maximum(entries, -reach), reach).astype(dtype)


def setup_inputs(seed: int = 0) -> dict:
    splits = jax.random.split(jax.random.key(seed), 7)
    activations = gaussian(splits[0], (TOKENS, D), 1.0, 6.0, ((0, 32), (1, 4)))
    cot_true = gaussian(splits[1], (TOKENS, KVW), 1.0, 6.0, ((0, 32), (1, 4)))
    cot_sampled = gaussian(splits[2], (TOKENS, KVW), 1.0, 6.0, ((0, 32), (1, 4)))
    tile_mask = draw_tile_mask(jax.random.fold_in(splits[6], 71), 0)
    moment = gaussian(splits[4], (D, KVW), (TOKENS * 625) ** -0.5, 0.0012207031, ((0, 32), (1, 4)), jnp.float32)
    curvature = jnp.clip(jnp.exp(math.log(3.0) - 6.9077553 * jax.random.uniform(splits[5], (D, KVW), jnp.float32) ** steps_of(splits[5], (D, KVW), ((0, 32), (1, 4)), -0.2, 0.2)), 0.003, 3.0)
    return dict(activations=activations, cot_true=cot_true, cot_sampled=cot_sampled, tile_mask=tile_mask, moment=moment, curvature=curvature)


BETA_ONE = 0.965
BETA_TWO = 0.99
GAMMA_CLIP = 0.01


def expand_tiles(tile_grid, tile_width):
    return jnp.repeat(jnp.repeat(tile_grid, tile_width, axis=0), tile_width, axis=1).astype(jnp.float32)


def reference(activations, cot_true, cot_sampled, tile_mask, moment, curvature):
    dense_mask = expand_tiles(tile_mask, BLOCK)
    inv_tokens = 1.0 / TOKENS
    contract = (((0,), (0,)), ((), ()))
    grad_true = lax.dot_general(activations, cot_true, contract, preferred_element_type=jnp.float32) * inv_tokens * dense_mask
    grad_sampled = lax.dot_general(activations, cot_sampled, contract, preferred_element_type=jnp.float32) * inv_tokens * dense_mask
    moment_new = BETA_ONE * moment + (1.0 - BETA_ONE) * grad_true
    hessian = TOKENS * grad_sampled * grad_sampled
    curvature_next = BETA_TWO * curvature + (1.0 - BETA_TWO) * hessian
    update = jnp.clip(moment_new / (GAMMA_CLIP * curvature_next), -1.0, 1.0) * dense_mask
    return update, curvature_next * dense_mask
```

```python
import functools

import jax
import jax.numpy as jnp
from jax import lax
from jax.experimental import pallas as pl
from jax.experimental.pallas import tpu as pltpu
from jax.sharding import PartitionSpec as P

D = 8192
BLOCK = 128
TOKENS = 32768

BETA_ONE = 0.965
BETA_TWO = 0.99
GAMMA_CLIP = 0.01
CONTRACT = (((0,), (0,)), ((), ()))
MESH = pl.DeviceIdType.MESH

SG = 26
HALF = SG // 2
TILE_ROWS = 16


def device_at(x, z, h, m):
    return (x * 8 + z * 2 + h, m)


def remote(src, dst, send_sem, recv_sem, device):
    return pltpu.make_async_remote_copy(
        src_ref=src, dst_ref=dst, send_sem=send_sem, recv_sem=recv_sem,
        device_id=device, device_id_type=MESH,
    )


def kernel(
    row_ref, col_ref, place_ref, acts_ref, true_ref, sampled_ref, out_ref,
    acts_t, near_cots, far_cots, part, relay1, final1, relay2, final2, mid, last, over_h, tiles, dense, landed,
    local_sem, pair_send, pair_recv, far_send, far_recv, fwd_send, fwd_recv,
    ring_send, ring_recv, h_send, h_recv, out_send, out_recv,
):
    dp = lax.axis_index("dp")
    m = lax.axis_index("mp")
    x, z, h = dp // 8, lax.rem(dp // 2, 4), lax.rem(dp, 2)
    l, core = m // 2, lax.rem(m, 2)
    pair = device_at(x, z, h, l * 2 + 1 - core)
    far = device_at(x, z, h, (1 - l) * 2 + core)
    up_x, down_x = lax.rem(x + 1, 4), lax.rem(x + 3, 4)
    up_z, down_z = lax.rem(z + 1, 4), lax.rem(z + 3, 4)
    along_x = (device_at(up_x, z, h, m), device_at(down_x, z, h, m))
    along_z = (device_at(x, up_z, h, m), device_at(x, down_z, h, m))
    across_h = device_at(x, z, 1 - h, m)

    barrier = pltpu.get_barrier_semaphore()
    for other in (pair, far, *along_x, *along_z, across_h):
        pl.semaphore_signal(barrier, inc=1, device_id=other, device_id_type=MESH)

    def greet(source, carry):
        @pl.when(jnp.logical_not(jnp.logical_and(source == dp, m == x)))
        def _():
            pl.semaphore_signal(barrier, inc=1, device_id=(source, x), device_id_type=MESH)
        return carry

    lax.fori_loop(0, 32, greet, 0)
    pl.semaphore_wait(barrier, jnp.where(m == x, 38, 39))

    def own(cc, g):
        return (true_ref, sampled_ref)[g].at[:, pl.ds(cc * BLOCK, BLOCK)]

    def place_of(cots, owner_core, cc, g):
        return cots.at[owner_core * 2 + cc, :, pl.ds(g * BLOCK, BLOCK)]

    pieces = [(cc, g) for cc in range(2) for g in range(2)]
    locals_, pairs, fars, fwds = [], [], [], []
    for i, (cc, g) in enumerate(pieces):
        here, there = place_of(near_cots, core, cc, g), place_of(far_cots, core, cc, g)
        fars.append(remote(own(cc, g), there, far_send.at[i], far_recv.at[i], far))
        pairs.append(remote(own(cc, g), here, pair_send.at[i], pair_recv.at[i], pair))
        locals_.append(pltpu.make_async_copy(own(cc, g), here, local_sem.at[i]))
    for copy in (*fars, *pairs, *locals_):
        copy.start()

    def transpose(r, carry):
        acts_t[r] = acts_ref[:, pl.ds(pl.multiple_of(r * BLOCK, BLOCK), BLOCK)].T
        return carry

    lax.fori_loop(0, TILE_ROWS, transpose, 0)

    def products(group):
        cots = (near_cots, far_cots)[group]

        def one(i, carry):
            for u in range(2):
                s = 2 * i + u
                row, col = row_ref[group * SG + s], col_ref[group * SG + s]
                tile = jnp.dot(acts_t[row], cots[col], preferred_element_type=jnp.float32)
                for g in range(2):
                    part[group, g, :, s] = tile[:, g * BLOCK : (g + 1) * BLOCK].reshape(16, 8, BLOCK)
            return carry

        lax.fori_loop(0, SG // 2, one, 0)

    def ring_open(ids, pos, neighbours, chunk, relay, final):
        send, recv = ring_send.at[ids], ring_recv.at[ids]
        up, down = neighbours
        opposite = lax.rem(pos + 2, 4)
        nxt, prv = lax.rem(pos + 1, 4), lax.rem(pos + 3, 4)
        copies = [
            remote(chunk(opposite, 0), relay.at[0], send.at[0], recv.at[0], up),
            remote(chunk(opposite, 1), relay.at[1], send.at[1], recv.at[1], down),
            remote(chunk(nxt, 1), final.at[0], send.at[2], recv.at[2], up),
            remote(chunk(prv, 0), final.at[1], send.at[3], recv.at[3], down),
            remote(relay.at[0], final.at[2], send.at[4], recv.at[4], up),
            remote(relay.at[1], final.at[3], send.at[5], recv.at[5], down),
        ]
        for copy in copies[:4]:
            copy.start()
        return copies

    def ring_turn(copies, pos, chunk, relay, add):
        nxt, prv = lax.rem(pos + 1, 4), lax.rem(pos + 3, 4)
        copies[0].wait_recv()
        add(relay.at[0], (relay.at[0], chunk(nxt, 0)))
        copies[4].start()
        copies[1].wait_recv()
        add(relay.at[1], (relay.at[1], chunk(prv, 1)))
        copies[5].start()

    def ring_close(copies, pos, chunk, final, add, result):
        for copy in copies[2:]:
            copy.wait_recv()
        add(result(0), (chunk(pos, 0), final.at[1], final.at[2]))
        add(result(1), (chunk(pos, 1), final.at[0], final.at[3]))

    def add_big(dst, srcs):
        for i in range(2):
            total = srcs[0][i] + srcs[1][i]
            for src in srcs[2:]:
                total = total + src[i]
            dst[i] = total

    def add_small(dst, srcs):
        total = srcs[0][...] + srcs[1][...]
        for src in srcs[2:]:
            total = total + src[...]
        dst[...] = total

    started = []

    def reduce_group(group):
        streams = ((x, along_x, z, along_z), (z, along_z, x, along_x))

        def chunk1(g):
            return lambda p, half: part.at[group, g, pl.ds(p * 4 + half * 2, 2)]

        def chunk2(g):
            return lambda p, half: mid.at[group, g, p, pl.ds(half * HALF, HALF)]

        first = []
        for g, (pos, near, _, _) in enumerate(streams):
            first.append(ring_open((group, g, 0), pos, near, chunk1(g), relay1.at[group, g], final1.at[group, g]))
        for g, (pos, _, _, _) in enumerate(streams):
            ring_turn(first[g], pos, chunk1(g), relay1.at[group, g], add_big)
        second = []
        for g, (pos, _, pos2, near2) in enumerate(streams):
            ring_close(
                first[g], pos, chunk1(g), final1.at[group, g], add_big,
                lambda half: mid.at[group, g, pl.ds(half * 2, 2)],
            )
            second.append(ring_open((group, g, 1), pos2, near2, chunk2(g), relay2.at[group, g], final2.at[group, g]))
        for g, (_, _, pos2, _) in enumerate(streams):
            ring_turn(second[g], pos2, chunk2(g), relay2.at[group, g], add_small)
        for g, (_, _, pos2, _) in enumerate(streams):
            ring_close(
                second[g], pos2, chunk2(g), final2.at[group, g], add_small,
                lambda half: last.at[group, g, pl.ds(half * HALF, HALF)],
            )
        swap = remote(
            last.at[group, 1 - h], over_h.at[group], h_send.at[group], h_recv.at[group], across_h
        )
        swap.start()
        for copies in (*first, *second):
            started.extend(copies)
        started.append(swap)
        swap.wait_recv()
        tiles[group, pl.ds(0, SG)] = last[group, h] + over_h[group]
        tiles[group, SG] = jnp.zeros((8, BLOCK), jnp.float32)

        columns = l if group == 0 else 1 - l

        def deliver(t, carry):
            for q in range(4):
                lo, cc = q // 2, q % 2
                row = (t // 2) * 2 + lo
                at = place_ref[group * 64 + row * 4 + lax.rem(t, 2) * 2 + cc]
                dense[group, t, q] = tiles[group, at]
            return carry

        lax.fori_loop(0, 16, deliver, 0)

        def owner(t):
            return m * 8 + t // 2, columns * 2 + lax.rem(t, 2)

        def itself(t):
            return jnp.logical_and(owner(t)[0] == dp, owner(t)[1] == m)

        def outgoing(t):
            return remote(dense.at[group, t], landed.at[dp], out_send.at[group, t], out_recv.at[dp], owner(t))

        def send(t, carry):
            @pl.when(itself(t))
            def _():
                pltpu.make_async_copy(dense.at[group, t], landed.at[dp], out_recv.at[dp]).start()

            @pl.when(jnp.logical_not(itself(t)))
            def _():
                outgoing(t).start()

            return carry

        def drain(t, carry):
            @pl.when(jnp.logical_not(itself(t)))
            def _():
                outgoing(t).wait_send()

            return carry

        lax.fori_loop(0, 16, send, 0)
        return drain

    for copy in (*locals_,):
        copy.wait()
    for copy in pairs:
        copy.wait_recv()
    products(0)
    drain0 = reduce_group(0)
    for i, (cc, g) in enumerate(pieces):
        fars[i].wait_recv()
        there = place_of(far_cots, core, cc, g)
        fwd = remote(there, there, fwd_send.at[i], fwd_recv.at[i], pair)
        fwd.start()
        fwds.append(fwd)
    for copy in fwds:
        copy.wait_recv()
    products(1)
    drain1 = reduce_group(1)

    def arrive(source, carry):
        pltpu.make_async_copy(landed.at[source], landed.at[source], out_recv.at[source]).wait()
        for q in range(4):
            lo, cc = q // 2, q % 2
            gx, gz, gh = source // 8, lax.rem(source // 2, 4), lax.rem(source, 2)
            strip = jnp.where(gh == 0, gx * 4 + gz, gz * 4 + gx)
            out_ref[
                gh, pl.ds(pl.multiple_of(lo * BLOCK + strip * 8, 8), 8), pl.ds(cc * BLOCK, BLOCK)
            ] = landed[source, q]
        return carry

    lax.fori_loop(0, 32, arrive, 0)

    for copy in (*fars, *pairs, *fwds, *started):
        copy.wait_send()
    lax.fori_loop(0, 16, drain0, 0)
    lax.fori_loop(0, 16, drain1, 0)


def reduced_tiles(rows, cols, places, activations, cot_true, cot_sampled):
    f32, bf16 = jnp.float32, jnp.bfloat16
    dma = pltpu.SemaphoreType.DMA
    vmem = pl.BlockSpec(memory_space=pltpu.VMEM)
    smem = pl.BlockSpec(memory_space=pltpu.SMEM)
    tokens = activations.shape[0]
    return pl.pallas_call(
        kernel,
        out_shape=jax.ShapeDtypeStruct((2, 2 * BLOCK, 2 * BLOCK), f32),
        in_specs=[smem, smem, smem, vmem, vmem, vmem],
        out_specs=vmem,
        scratch_shapes=[
            pltpu.VMEM((TILE_ROWS, BLOCK, tokens), bf16),
            pltpu.VMEM((4, tokens, 2 * BLOCK), bf16),
            pltpu.VMEM((4, tokens, 2 * BLOCK), bf16),
            pltpu.VMEM((2, 2, 16, SG, 8, BLOCK), f32),
            pltpu.VMEM((2, 2, 2, 2, SG, 8, BLOCK), f32),
            pltpu.VMEM((2, 2, 4, 2, SG, 8, BLOCK), f32),
            pltpu.VMEM((2, 2, 2, HALF, 8, BLOCK), f32),
            pltpu.VMEM((2, 2, 4, HALF, 8, BLOCK), f32),
            pltpu.VMEM((2, 2, 4, SG, 8, BLOCK), f32),
            pltpu.VMEM((2, 2, SG, 8, BLOCK), f32),
            pltpu.VMEM((2, SG, 8, BLOCK), f32),
            pltpu.VMEM((2, SG + 1, 8, BLOCK), f32),
            pltpu.VMEM((2, 16, 4, 8, BLOCK), f32),
            pltpu.VMEM((32, 4, 8, BLOCK), f32),
            dma((4,)), dma((4,)), dma((4,)), dma((4,)), dma((4,)), dma((4,)), dma((4,)),
            dma((2, 2, 2, 6)), dma((2, 2, 2, 6)), dma((2,)), dma((2,)), dma((2, 16)), dma((32,)),
        ],
        compiler_params=pltpu.CompilerParams(
            collective_id=0, has_side_effects=True, vmem_limit_bytes=60 << 20
        ),
        name="reduced_tiles",
    )(rows, cols, places, activations, cot_true, cot_sampled)


def tables(tile_mask, m, round_):
    own_rows = lax.dynamic_slice_in_dim(tile_mask, m * TILE_ROWS, TILE_ROWS, 0)
    halves = own_rows.reshape(TILE_ROWS, 2, 4)
    halves = jnp.where(m < 2, halves, halves[:, ::-1])
    kept = halves.transpose(1, 0, 2).reshape(2, 64) > 0
    index = jnp.arange(64)
    before = jnp.sum(kept[:, None, :] & (index[None, :] < index[:, None])[None], axis=2)
    slot = before - round_ * SG
    here = kept & (slot >= 0) & (slot < SG)
    places = jnp.where(here, slot, SG).astype(jnp.int32).reshape(-1)
    chosen = here[:, None, :] & (slot[:, None, :] == jnp.arange(SG)[None, :, None])
    def listed(values):
        return jnp.sum(jnp.where(chosen, values[:, None, :], 0), axis=2).astype(jnp.int32).reshape(-1)

    rows, cols = listed((index // 4)[None, :]), listed((index % 4)[None, :])
    return rows, cols, places


def on_device(activations, cot_true, cot_sampled, tile_mask, moment, curvature):
    m = lax.axis_index("mp")
    dp = lax.axis_index("dp")
    tokens_all = activations.shape[0] * lax.axis_size("dp")
    counts = jnp.sum(tile_mask.reshape(4, TILE_ROWS, 2, 4) > 0, axis=(1, 3))
    rounds = (jnp.max(counts) + SG - 1) // SG

    def step(state):
        round_, total = state
        rows, cols, places = tables(tile_mask, m, round_)
        return round_ + 1, total + reduced_tiles(rows, cols, places, activations, cot_true, cot_sampled)

    start = (jnp.int32(0), jnp.zeros((2, 2 * BLOCK, 2 * BLOCK), jnp.float32))
    _, sums = lax.while_loop(lambda state: state[0] < rounds, step, start)
    owned = lax.dynamic_slice(tile_mask, (dp * 2, m * 2), (2, 2))
    owned_mask = jnp.repeat(jnp.repeat(owned, BLOCK, axis=0), BLOCK, axis=1).astype(jnp.float32)
    grads = sums * (1.0 / tokens_all)
    moment_new = BETA_ONE * moment + (1.0 - BETA_ONE) * grads[0]
    hessian = tokens_all * grads[1] * grads[1]
    curvature_next = BETA_TWO * curvature + (1.0 - BETA_TWO) * hessian
    update = jnp.clip(moment_new / (GAMMA_CLIP * curvature_next), -1.0, 1.0) * owned_mask
    return (update, curvature_next * owned_mask)


def solution(mesh):
    return jax.shard_map(
        on_device,
        mesh=mesh,
        in_specs=(P("dp", "mp"), P("dp", "mp"), P("dp", "mp"), P(), P("dp", "mp"), P("dp", "mp")),
        out_specs=(P("dp", "mp"), P("dp", "mp")),
        check_vma=False,
    )
```

```python
import jax
import jax.numpy as jnp
from jax import lax
from jax.experimental import pallas as pl
from jax.experimental.pallas import tpu as pltpu
from jax.sharding import PartitionSpec as P

D = 8192
BLOCK = 128
BETA_ONE = 0.965
BETA_TWO = 0.99
GAMMA_CLIP = 0.01
MESH = pl.DeviceIdType.MESH
F32, BF16, I32 = jnp.float32, jnp.bfloat16, jnp.int32

GROUP_COLS = (4, 2, 2)
WAVES = ((0, 0, 14), (0, 14, 12), (1, 0, 16), (2, 0, 16))
GROUP_SLOTS = tuple(sum(n for g, _, n in WAVES if g == group) for group in range(3))
TILE_ROWS = 16

ROWS_AT, COLS_AT, PLACES_AT = [], [], []
TABLE_SIZE = 0
for _slots, _cols in zip(GROUP_SLOTS, GROUP_COLS):
    ROWS_AT.append(TABLE_SIZE)
    COLS_AT.append(TABLE_SIZE + _slots)
    PLACES_AT.append(TABLE_SIZE + 2 * _slots)
    TABLE_SIZE += 2 * _slots + TILE_ROWS * _cols


def remote(src, dst, send_sem, recv_sem, device):
    return pltpu.make_async_remote_copy(
        src_ref=src, dst_ref=dst, send_sem=send_sem, recv_sem=recv_sem,
        device_id=device, device_id_type=MESH,
    )


def scratch_list(tokens):
    dma = pltpu.SemaphoreType.DMA
    shapes = dict(
        acts=pltpu.VMEM((tokens, TILE_ROWS * BLOCK), BF16),
        acts_t=pltpu.VMEM((TILE_ROWS, BLOCK, tokens), BF16),
        landed=pltpu.VMEM((32, 2, 2, 8, BLOCK), F32),
        in_sem=dma((7,)),
        pair_send=dma((4,)), pair_recv=dma((4,)),
        far_send=dma((4,)), far_recv=dma((4,)),
        fwd_send=dma((4,)), fwd_recv=dma((4,)),
    )
    for g, cols in enumerate(GROUP_COLS):
        n = GROUP_SLOTS[g]
        shapes[f"cots{g}"] = pltpu.VMEM((cols, tokens, 2 * BLOCK), BF16)
        shapes[f"tiles{g}"] = pltpu.VMEM((n + 1, 8, BLOCK), F32)
        per_owner = (2, 2) if g == 0 else (2,)
        shapes[f"dense{g}"] = pltpu.VMEM((16, *per_owner, 8, BLOCK), F32)
        shapes[f"out_send{g}"] = dma((16,))
        shapes[f"out_recv{g}"] = dma((32,))
    for w, (_, _, n) in enumerate(WAVES):
        half = n // 2
        shapes[f"part{w}"] = pltpu.VMEM((2, 16, n, 8, BLOCK), F32)
        shapes[f"relay1_{w}"] = pltpu.VMEM((2, 2, 2, n, 8, BLOCK), F32)
        shapes[f"final1_{w}"] = pltpu.VMEM((2, 4, 2, n, 8, BLOCK), F32)
        shapes[f"relay2_{w}"] = pltpu.VMEM((2, 2, half, 8, BLOCK), F32)
        shapes[f"final2_{w}"] = pltpu.VMEM((2, 4, half, 8, BLOCK), F32)
        shapes[f"mid{w}"] = pltpu.VMEM((2, 4, n, 8, BLOCK), F32)
        shapes[f"last{w}"] = pltpu.VMEM((2, n, 8, BLOCK), F32)
        shapes[f"over{w}"] = pltpu.VMEM((n, 8, BLOCK), F32)
        shapes[f"ring_send{w}"] = dma((2, 2, 6))
        shapes[f"ring_recv{w}"] = dma((2, 2, 6))
        shapes[f"swap_send{w}"] = dma((1,))
        shapes[f"swap_recv{w}"] = dma((1,))
    return shapes


def kernel(*refs):
    refs = list(refs)
    names = list(scratch_list(8))
    r = dict(zip(names, refs[-len(names):]))
    table_ref, acts_hbm, true_ref, sampled_ref, out_ref = refs[: -len(names)]

    dp = lax.axis_index("dp")
    m = lax.axis_index("mp")
    x, z, h = dp // 8, lax.rem(dp // 2, 4), lax.rem(dp, 2)
    l, core = m // 2, lax.rem(m, 2)

    def device_at(x, z, h, m):
        return (x * 8 + z * 2 + h, m)

    pair = device_at(x, z, h, l * 2 + 1 - core)
    far = device_at(x, z, h, (1 - l) * 2 + core)
    along_x = [device_at(lax.rem(x + d, 4), z, h, m) for d in (1, 3)]
    along_z = [device_at(x, lax.rem(z + d, 4), h, m) for d in (1, 3)]
    across_h = device_at(x, z, 1 - h, m)

    acts_in = pltpu.make_async_copy(acts_hbm, r["acts"], r["in_sem"].at[0])
    acts_in.start()

    barrier = pltpu.get_barrier_semaphore()
    for other in (pair, far, *along_x, *along_z, across_h):
        pl.semaphore_signal(barrier, inc=1, device_id=other, device_id_type=MESH)

    def greet(sender, carry):
        @pl.when(jnp.logical_not(jnp.logical_and(sender == dp, m == x)))
        def _():
            pl.semaphore_signal(barrier, inc=1, device_id=(sender, x), device_id_type=MESH)
        return carry

    lax.fori_loop(0, 32, greet, 0)
    pl.semaphore_wait(barrier, jnp.where(m == x, 38, 39))

    def own(cc, g):
        return (true_ref, sampled_ref)[g].at[:, pl.ds(cc * BLOCK, BLOCK)]

    def lanes(g):
        return pl.ds(g * BLOCK, BLOCK)

    pieces = [(cc, g) for cc in range(2) for g in range(2)]
    inputs, pairs, fars, fwds, started = [], [], [], [], []
    for i, (cc, g) in enumerate(pieces):
        near_place = r["cots0"].at[core * 2 + cc, :, lanes(g)]
        far_place = r[f"cots{1 + cc}"].at[core, :, lanes(g)]
        fars.append(remote(own(cc, g), far_place, r["far_send"].at[i], r["far_recv"].at[i], far))
        pairs.append(remote(own(cc, g), near_place, r["pair_send"].at[i], r["pair_recv"].at[i], pair))
        inputs.append(pltpu.make_async_copy(own(cc, g), near_place, r["in_sem"].at[1 + i]))
    for copies in (fars, pairs, inputs):
        for copy in copies:
            copy.start()
    acts_in.wait()

    def transpose(row, carry):
        r["acts_t"][row] = r["acts"][:, pl.ds(pl.multiple_of(row * BLOCK, BLOCK), BLOCK)].T
        return carry

    lax.fori_loop(0, TILE_ROWS, transpose, 0)

    def products(w):
        group, first, n = WAVES[w]
        cots, part = r[f"cots{group}"], r[f"part{w}"]

        def one(i, carry):
            for u in range(2):
                s = 2 * i + u
                row = table_ref[ROWS_AT[group] + first + s]
                col = table_ref[COLS_AT[group] + first + s]
                tile = jnp.dot(r["acts_t"][row], cots[col], preferred_element_type=F32)
                for g in range(2):
                    part[g, :, s] = tile[:, g * BLOCK : (g + 1) * BLOCK].reshape(16, 8, BLOCK)
            return carry

        lax.fori_loop(0, n // 2, one, 0)

    def ring_open(send, recv, pos, neighbours, chunk, relay, final):
        up, down = neighbours
        nxt, opposite, prv = (lax.rem(pos + d, 4) for d in (1, 2, 3))
        copies = [
            remote(chunk(opposite, 0), relay.at[0], send.at[0], recv.at[0], up),
            remote(chunk(opposite, 1), relay.at[1], send.at[1], recv.at[1], down),
            remote(chunk(nxt, 1), final.at[0], send.at[2], recv.at[2], up),
            remote(chunk(prv, 0), final.at[1], send.at[3], recv.at[3], down),
            remote(relay.at[0], final.at[2], send.at[4], recv.at[4], up),
            remote(relay.at[1], final.at[3], send.at[5], recv.at[5], down),
        ]
        for copy in copies[:4]:
            copy.start()
        started.extend(copies)
        return copies

    def ring_turn(copies, pos, chunk, relay, add):
        for i, d in enumerate((1, 3)):
            copies[i].wait_recv()
            add(relay.at[i], (relay.at[i], chunk(lax.rem(pos + d, 4), i)))
            copies[4 + i].start()

    def ring_close(copies, pos, chunk, final, add, result):
        for copy in copies[2:]:
            copy.wait_recv()
        add(result(0), (chunk(pos, 0), final.at[1], final.at[2]))
        add(result(1), (chunk(pos, 1), final.at[0], final.at[3]))

    def add_big(dst, srcs):
        for i in range(2):
            total = srcs[0][i] + srcs[1][i]
            for src in srcs[2:]:
                total = total + src[i]
            dst[i] = total

    def add_small(dst, srcs):
        total = srcs[0][...] + srcs[1][...]
        for src in srcs[2:]:
            total = total + src[...]
        dst[...] = total

    streams = ((x, along_x, z, along_z), (z, along_z, x, along_x))
    first_ring, second_ring, swaps = {}, {}, {}

    def chunk1(w, s):
        return lambda p, half: r[f"part{w}"].at[s, pl.ds(p * 4 + half * 2, 2)]

    def chunk2(w, s):
        half_n = WAVES[w][2] // 2
        return lambda p, half: r[f"mid{w}"].at[s, p, pl.ds(half * half_n, half_n)]

    def open_first(w):
        for s, (pos, near, _, _) in enumerate(streams):
            first_ring[w, s] = ring_open(
                r[f"ring_send{w}"].at[s, 0], r[f"ring_recv{w}"].at[s, 0], pos, near, chunk1(w, s),
                r[f"relay1_{w}"].at[s], r[f"final1_{w}"].at[s],
            )

    def turn_first(w):
        for s, (pos, _, _, _) in enumerate(streams):
            ring_turn(first_ring[w, s], pos, chunk1(w, s), r[f"relay1_{w}"].at[s], add_big)

    def close_first(w):
        for s, (pos, _, pos2, near2) in enumerate(streams):
            ring_close(
                first_ring[w, s], pos, chunk1(w, s), r[f"final1_{w}"].at[s], add_big,
                lambda half: r[f"mid{w}"].at[s, pl.ds(half * 2, 2)],
            )
            second_ring[w, s] = ring_open(
                r[f"ring_send{w}"].at[s, 1], r[f"ring_recv{w}"].at[s, 1], pos2, near2, chunk2(w, s),
                r[f"relay2_{w}"].at[s], r[f"final2_{w}"].at[s],
            )

    def turn_second(w):
        for s, (_, _, pos2, _) in enumerate(streams):
            ring_turn(second_ring[w, s], pos2, chunk2(w, s), r[f"relay2_{w}"].at[s], add_small)

    def close_second(w):
        half_n = WAVES[w][2] // 2
        for s, (_, _, pos2, _) in enumerate(streams):
            ring_close(
                second_ring[w, s], pos2, chunk2(w, s), r[f"final2_{w}"].at[s], add_small,
                lambda half: r[f"last{w}"].at[s, pl.ds(half * half_n, half_n)],
            )
        swaps[w] = remote(
            r[f"last{w}"].at[1 - h], r[f"over{w}"], r[f"swap_send{w}"].at[0], r[f"swap_recv{w}"].at[0], across_h
        )
        swaps[w].start()
        started.append(swaps[w])

    def owner(g, t):
        return m * 8 + t // 2, (l if g == 0 else 1 - l) * 2 + lax.rem(t, 2)

    def itself(g, t):
        return jnp.logical_and(owner(g, t)[0] == dp, owner(g, t)[1] == m)

    def spot(g):
        return r["landed"].at[dp] if g == 0 else r["landed"].at[dp, g - 1]

    def outgoing(g, t):
        return remote(r[f"dense{g}"].at[t], spot(g), r[f"out_send{g}"].at[t], r[f"out_recv{g}"].at[dp], owner(g, t))

    def deliver(g):
        tiles, dense = r[f"tiles{g}"], r[f"dense{g}"]
        for w, (group, first, n) in enumerate(WAVES):
            if group == g:
                swaps[w].wait_recv()
                tiles[pl.ds(first, n)] = r[f"last{w}"][h] + r[f"over{w}"][...]
        tiles[GROUP_SLOTS[g]] = jnp.zeros((8, BLOCK), F32)

        def one(t, carry):
            core_to = lax.rem(t, 2)
            for lo in range(2):
                row = (t // 2) * 2 + lo
                if g == 0:
                    for cc in range(2):
                        dense[t, cc, lo] = tiles[table_ref[PLACES_AT[g] + row * 4 + core_to * 2 + cc]]
                else:
                    dense[t, lo] = tiles[table_ref[PLACES_AT[g] + row * 2 + core_to]]

            @pl.when(itself(g, t))
            def _():
                pltpu.make_async_copy(dense.at[t], spot(g), r[f"out_recv{g}"].at[dp]).start()

            @pl.when(jnp.logical_not(itself(g, t)))
            def _():
                outgoing(g, t).start()

            return carry

        lax.fori_loop(0, 16, one, 0)

    def drain(g):
        def one(t, carry):
            @pl.when(jnp.logical_not(itself(g, t)))
            def _():
                outgoing(g, t).wait_send()

            return carry

        lax.fori_loop(0, 16, one, 0)

    def forward(cc):
        for i, (piece_cc, g) in enumerate(pieces):
            if piece_cc == cc:
                fars[i].wait_recv()
                place = r[f"cots{1 + cc}"].at[core, :, lanes(g)]
                copy = remote(place, place, r["fwd_send"].at[i], r["fwd_recv"].at[i], pair)
                copy.start()
                fwds.append(copy)

    def forwarded(cc):
        for copy in fwds[cc * 2 : cc * 2 + 2]:
            copy.wait_recv()

    for copy in inputs:
        copy.wait()
    for copy in pairs:
        copy.wait_recv()
    products(0)
    open_first(0)
    products(1)
    open_first(1)
    turn_first(0)
    forward(0)
    turn_first(1)
    forwarded(0)
    products(2)
    open_first(2)
    close_first(0)
    close_first(1)
    turn_first(2)
    forward(1)
    forwarded(1)
    products(3)
    open_first(3)
    turn_second(0)
    turn_second(1)
    close_second(0)
    close_second(1)
    close_first(2)
    turn_first(3)
    turn_second(2)
    deliver(0)
    close_second(2)
    close_first(3)
    deliver(1)
    turn_second(3)
    close_second(3)
    deliver(2)

    def arrived(g):
        def one(i, carry):
            place = r["landed"].at[i] if g == 0 else r["landed"].at[i, g - 1]
            pltpu.make_async_copy(place, place, r[f"out_recv{g}"].at[i]).wait()
            return carry

        lax.fori_loop(0, 32, one, 0)

    @pl.when(m // 2 == x // 2)
    def _():
        arrived(0)

    @pl.when(m // 2 != x // 2)
    def _():
        arrived(1)
        arrived(2)

    def finish(strip, carry):
        from_true = strip * 2
        from_sampled = (lax.rem(strip, 4) * 4 + strip // 4) * 2 + 1
        for cc in range(2):
            for lo in range(2):
                at = (pl.ds(pl.multiple_of(lo * BLOCK + strip * 8, 8), 8), pl.ds(cc * BLOCK, BLOCK))
                out_ref[(0, *at)] = r["landed"][from_true, cc, lo]
                out_ref[(1, *at)] = r["landed"][from_sampled, cc, lo]
        return carry

    lax.fori_loop(0, 16, finish, 0)

    for copy in (*fars, *pairs, *fwds, *started):
        copy.wait_send()
    for g in range(3):
        drain(g)


def reduced_tiles(table, activations, cot_true, cot_sampled):
    vmem = pl.BlockSpec(memory_space=pltpu.VMEM)
    smem = pl.BlockSpec(memory_space=pltpu.SMEM)
    hbm = pl.BlockSpec(memory_space=pl.ANY)
    return pl.pallas_call(
        kernel,
        out_shape=jax.ShapeDtypeStruct((2, 2 * BLOCK, 2 * BLOCK), F32),
        in_specs=[smem, hbm, hbm, hbm],
        out_specs=vmem,
        scratch_shapes=list(scratch_list(activations.shape[0]).values()),
        compiler_params=pltpu.CompilerParams(
            collective_id=0, has_side_effects=True, vmem_limit_bytes=60 << 20
        ),
        name="reduced_tiles",
    )(table, activations, cot_true, cot_sampled)


def group_columns(half, group):
    if group == 0:
        return tuple(half * 4 + k for k in range(4))
    return tuple((1 - half) * 4 + k * 2 + group - 1 for k in range(2))


def tables(tile_mask, m, round_):
    own_rows = lax.dynamic_slice_in_dim(tile_mask, m * TILE_ROWS, TILE_ROWS, 0) > 0
    parts = []
    for group, n in enumerate(GROUP_SLOTS):
        first, second = (own_rows[:, jnp.array(group_columns(half, group))] for half in range(2))
        kept = jnp.where(m < 2, first, second).reshape(-1)
        cols = GROUP_COLS[group]
        index = jnp.arange(TILE_ROWS * cols)
        slot = jnp.sum(kept[None, :] & (index[None, :] < index[:, None]), axis=1) - round_ * n
        here = kept & (slot >= 0) & (slot < n)
        chosen = here[None, :] & (slot[None, :] == jnp.arange(n)[:, None])
        parts.append(jnp.sum(jnp.where(chosen, index[None, :] // cols, 0), axis=1))
        parts.append(jnp.sum(jnp.where(chosen, index[None, :] % cols, 0), axis=1))
        parts.append(jnp.where(here, slot, n))
    return jnp.concatenate(parts).astype(I32)


def rounds_of(tile_mask):
    counts = jnp.sum(tile_mask.reshape(4, TILE_ROWS, 8) > 0, axis=1)
    rounds = jnp.int32(1)
    for source in range(4):
        for group, n in enumerate(GROUP_SLOTS):
            filled = sum(counts[source, col] for col in group_columns(source // 2, group))
            rounds = jnp.maximum(rounds, (filled + n - 1) // n)
    return rounds


def on_device(activations, cot_true, cot_sampled, tile_mask, moment, curvature):
    m = lax.axis_index("mp")
    dp = lax.axis_index("dp")
    tokens_all = activations.shape[0] * lax.axis_size("dp")
    rounds = rounds_of(tile_mask)

    def step(state):
        round_, total = state
        table = tables(tile_mask, m, round_)
        return round_ + 1, total + reduced_tiles(table, activations, cot_true, cot_sampled)

    start = (jnp.int32(0), jnp.zeros((2, 2 * BLOCK, 2 * BLOCK), jnp.float32))
    _, sums = lax.while_loop(lambda state: state[0] < rounds, step, start)
    owned = lax.dynamic_slice(tile_mask, (dp * 2, m * 2), (2, 2))
    owned_mask = jnp.repeat(jnp.repeat(owned, BLOCK, axis=0), BLOCK, axis=1).astype(jnp.float32)
    grads = sums * (1.0 / tokens_all)
    moment_new = BETA_ONE * moment + (1.0 - BETA_ONE) * grads[0]
    hessian = tokens_all * grads[1] * grads[1]
    curvature_next = BETA_TWO * curvature + (1.0 - BETA_TWO) * hessian
    update = jnp.clip(moment_new / (GAMMA_CLIP * curvature_next), -1.0, 1.0) * owned_mask
    return (update, curvature_next * owned_mask)


def solution(mesh):
    return jax.shard_map(
        on_device,
        mesh=mesh,
        in_specs=(P("dp", "mp"), P("dp", "mp"), P("dp", "mp"), P(), P("dp", "mp"), P("dp", "mp")),
        out_specs=(P("dp", "mp"), P("dp", "mp")),
        check_vma=False,
    )
```

```python
import functools

import jax
import jax.numpy as jnp
from jax import lax
from jax.experimental import pallas as pl
from jax.experimental.pallas import tpu as pltpu
from jax.sharding import PartitionSpec as P

D = 8192
BLOCK = 128
BETA_ONE = 0.965
BETA_TWO = 0.99
GAMMA_CLIP = 0.01
MESH = pl.DeviceIdType.MESH
F32, BF16, I32 = jnp.float32, jnp.bfloat16, jnp.int32

GROUP_COLS = (4, 2, 2)
WAVES = ((0, 0, 14), (0, 14, 12), (1, 0, 16), (2, 0, 16))
GROUP_SLOTS = tuple(sum(n for g, _, n in WAVES if g == group) for group in range(3))
TILE_ROWS = 16

FIRST_COL = (0, 4, 6)
LIST_AT = TILE_ROWS
ROUNDS_AT = TILE_ROWS + 6
TABLE = (TILE_ROWS + 8, BLOCK)


def remote(src, dst, send_sem, recv_sem, device):
    return pltpu.make_async_remote_copy(
        src_ref=src, dst_ref=dst, send_sem=send_sem, recv_sem=recv_sem,
        device_id=device, device_id_type=MESH,
    )


def scratch_list(tokens):
    dma = pltpu.SemaphoreType.DMA
    shapes = dict(
        moment=pltpu.VMEM((2 * BLOCK, 2 * BLOCK), F32),
        curvature=pltpu.VMEM((2 * BLOCK, 2 * BLOCK), F32),
        acts=pltpu.VMEM((tokens, TILE_ROWS * BLOCK), BF16),
        acts_t=pltpu.VMEM((TILE_ROWS, BLOCK, tokens), BF16),
        landed=pltpu.VMEM((32, 2, 2, 8, BLOCK), F32),
        in_sem=dma((7,)),
        pair_send=dma((4,)), pair_recv=dma((4,)),
        far_send=dma((4,)), far_recv=dma((4,)),
        fwd_send=dma((4,)), fwd_recv=dma((4,)),
    )
    for g, cols in enumerate(GROUP_COLS):
        n = GROUP_SLOTS[g]
        shapes[f"cots{g}"] = pltpu.VMEM((cols, tokens, 2 * BLOCK), BF16)
        shapes[f"tiles{g}"] = pltpu.VMEM((n + 1, 8, BLOCK), F32)
        per_owner = (2, 2) if g == 0 else (2,)
        shapes[f"dense{g}"] = pltpu.VMEM((16, *per_owner, 8, BLOCK), F32)
        shapes[f"out_send{g}"] = dma((16,))
        shapes[f"out_recv{g}"] = dma((32,))
    for w, (_, _, n) in enumerate(WAVES):
        half = n // 2
        shapes[f"part{w}"] = pltpu.VMEM((2, 16, n, 8, BLOCK), F32)
        shapes[f"relay1_{w}"] = pltpu.VMEM((2, 2, 2, n, 8, BLOCK), F32)
        shapes[f"final1_{w}"] = pltpu.VMEM((2, 4, 2, n, 8, BLOCK), F32)
        shapes[f"relay2_{w}"] = pltpu.VMEM((2, 2, half, 8, BLOCK), F32)
        shapes[f"final2_{w}"] = pltpu.VMEM((2, 4, half, 8, BLOCK), F32)
        shapes[f"mid{w}"] = pltpu.VMEM((2, 4, n, 8, BLOCK), F32)
        shapes[f"last{w}"] = pltpu.VMEM((2, n, 8, BLOCK), F32)
        shapes[f"over{w}"] = pltpu.VMEM((n, 8, BLOCK), F32)
        shapes[f"ring_send{w}"] = dma((2, 2, 6))
        shapes[f"ring_recv{w}"] = dma((2, 2, 6))
        shapes[f"swap_send{w}"] = dma((1,))
        shapes[f"swap_recv{w}"] = dma((1,))
    return shapes


def kernel(tokens_all, *refs):
    refs = list(refs)
    names = list(scratch_list(8))
    r = dict(zip(names, refs[-len(names):]))
    table_ref, mask_ref, acts_hbm, true_ref, sampled_ref, moment_hbm, curvature_hbm, sums_in = refs[:8]
    update_ref, new_curvature_ref, sums_ref = refs[8 : -len(names)]

    dp = lax.axis_index("dp")
    m = lax.axis_index("mp")
    x, z, h = dp // 8, lax.rem(dp // 2, 4), lax.rem(dp, 2)
    l, core = m // 2, lax.rem(m, 2)

    def device_at(x, z, h, m):
        return (x * 8 + z * 2 + h, m)

    pair = device_at(x, z, h, l * 2 + 1 - core)
    far = device_at(x, z, h, (1 - l) * 2 + core)
    along_x = [device_at(lax.rem(x + d, 4), z, h, m) for d in (1, 3)]
    along_z = [device_at(x, lax.rem(z + d, 4), h, m) for d in (1, 3)]
    across_h = device_at(x, z, 1 - h, m)

    acts_in = pltpu.make_async_copy(acts_hbm, r["acts"], r["in_sem"].at[0])
    acts_in.start()

    barrier = pltpu.get_barrier_semaphore()
    for other in (pair, far, *along_x, *along_z, across_h):
        pl.semaphore_signal(barrier, inc=1, device_id=other, device_id_type=MESH)

    def greet(sender, carry):
        @pl.when(jnp.logical_not(jnp.logical_and(sender == dp, m == x)))
        def _():
            pl.semaphore_signal(barrier, inc=1, device_id=(sender, x), device_id_type=MESH)
        return carry

    lax.fori_loop(0, 32, greet, 0)
    pl.semaphore_wait(barrier, jnp.where(m == x, 38, 39))

    def own(cc, g):
        return (true_ref, sampled_ref)[g].at[:, pl.ds(cc * BLOCK, BLOCK)]

    def lanes(g):
        return pl.ds(g * BLOCK, BLOCK)

    pieces = [(cc, g) for cc in range(2) for g in range(2)]
    inputs, pairs, fars, fwds, started = [], [], [], [], []
    for i, (cc, g) in enumerate(pieces):
        near_place = r["cots0"].at[core * 2 + cc, :, lanes(g)]
        far_place = r[f"cots{1 + cc}"].at[core, :, lanes(g)]
        fars.append(remote(own(cc, g), far_place, r["far_send"].at[i], r["far_recv"].at[i], far))
        pairs.append(remote(own(cc, g), near_place, r["pair_send"].at[i], r["pair_recv"].at[i], pair))
        inputs.append(pltpu.make_async_copy(own(cc, g), near_place, r["in_sem"].at[1 + i]))
    for copies in (fars, pairs, inputs):
        for copy in copies:
            copy.start()
    moment_in = pltpu.make_async_copy(moment_hbm, r["moment"], r["in_sem"].at[5])
    curvature_in = pltpu.make_async_copy(curvature_hbm, r["curvature"], r["in_sem"].at[6])
    moment_in.start()
    curvature_in.start()
    acts_in.wait()

    def transpose(row, carry):
        r["acts_t"][row] = r["acts"][:, pl.ds(pl.multiple_of(row * BLOCK, BLOCK), BLOCK)].T
        return carry

    lax.fori_loop(0, TILE_ROWS, transpose, 0)

    def products(w):
        group, first, n = WAVES[w]
        cots, part = r[f"cots{group}"], r[f"part{w}"]

        def one(i, carry):
            for u in range(2):
                s = 2 * i + u
                row = table_ref[LIST_AT + 2 * group, first + s]
                col = table_ref[LIST_AT + 2 * group + 1, first + s]
                tile = jnp.dot(r["acts_t"][row], cots[col], preferred_element_type=F32)
                for g in range(2):
                    part[g, :, s] = tile[:, g * BLOCK : (g + 1) * BLOCK].reshape(16, 8, BLOCK)
            return carry

        lax.fori_loop(0, n // 2, one, 0)

    def ring_open(send, recv, pos, neighbours, chunk, relay, final):
        up, down = neighbours
        nxt, opposite, prv = (lax.rem(pos + d, 4) for d in (1, 2, 3))
        copies = [
            remote(chunk(opposite, 0), relay.at[0], send.at[0], recv.at[0], up),
            remote(chunk(opposite, 1), relay.at[1], send.at[1], recv.at[1], down),
            remote(chunk(nxt, 1), final.at[0], send.at[2], recv.at[2], up),
            remote(chunk(prv, 0), final.at[1], send.at[3], recv.at[3], down),
            remote(relay.at[0], final.at[2], send.at[4], recv.at[4], up),
            remote(relay.at[1], final.at[3], send.at[5], recv.at[5], down),
        ]
        for copy in copies[:4]:
            copy.start()
        started.extend(copies)
        return copies

    def ring_turn(copies, pos, chunk, relay, add):
        for i, d in enumerate((1, 3)):
            copies[i].wait_recv()
            add(relay.at[i], (relay.at[i], chunk(lax.rem(pos + d, 4), i)))
            copies[4 + i].start()

    def ring_close(copies, pos, chunk, final, add, result):
        for copy in copies[2:]:
            copy.wait_recv()
        add(result(0), (chunk(pos, 0), final.at[1], final.at[2]))
        add(result(1), (chunk(pos, 1), final.at[0], final.at[3]))

    def add_big(dst, srcs):
        for i in range(2):
            total = srcs[0][i] + srcs[1][i]
            for src in srcs[2:]:
                total = total + src[i]
            dst[i] = total

    def add_small(dst, srcs):
        total = srcs[0][...] + srcs[1][...]
        for src in srcs[2:]:
            total = total + src[...]
        dst[...] = total

    streams = ((x, along_x, z, along_z), (z, along_z, x, along_x))
    first_ring, second_ring, swaps = {}, {}, {}

    def chunk1(w, s):
        return lambda p, half: r[f"part{w}"].at[s, pl.ds(p * 4 + half * 2, 2)]

    def chunk2(w, s):
        half_n = WAVES[w][2] // 2
        return lambda p, half: r[f"mid{w}"].at[s, p, pl.ds(half * half_n, half_n)]

    def open_first(w):
        for s, (pos, near, _, _) in enumerate(streams):
            first_ring[w, s] = ring_open(
                r[f"ring_send{w}"].at[s, 0], r[f"ring_recv{w}"].at[s, 0], pos, near, chunk1(w, s),
                r[f"relay1_{w}"].at[s], r[f"final1_{w}"].at[s],
            )

    def turn_first(w):
        for s, (pos, _, _, _) in enumerate(streams):
            ring_turn(first_ring[w, s], pos, chunk1(w, s), r[f"relay1_{w}"].at[s], add_big)

    def close_first(w):
        for s, (pos, _, pos2, near2) in enumerate(streams):
            ring_close(
                first_ring[w, s], pos, chunk1(w, s), r[f"final1_{w}"].at[s], add_big,
                lambda half: r[f"mid{w}"].at[s, pl.ds(half * 2, 2)],
            )
            second_ring[w, s] = ring_open(
                r[f"ring_send{w}"].at[s, 1], r[f"ring_recv{w}"].at[s, 1], pos2, near2, chunk2(w, s),
                r[f"relay2_{w}"].at[s], r[f"final2_{w}"].at[s],
            )

    def turn_second(w):
        for s, (_, _, pos2, _) in enumerate(streams):
            ring_turn(second_ring[w, s], pos2, chunk2(w, s), r[f"relay2_{w}"].at[s], add_small)

    def close_second(w):
        half_n = WAVES[w][2] // 2
        for s, (_, _, pos2, _) in enumerate(streams):
            ring_close(
                second_ring[w, s], pos2, chunk2(w, s), r[f"final2_{w}"].at[s], add_small,
                lambda half: r[f"last{w}"].at[s, pl.ds(half * half_n, half_n)],
            )
        swaps[w] = remote(
            r[f"last{w}"].at[1 - h], r[f"over{w}"], r[f"swap_send{w}"].at[0], r[f"swap_recv{w}"].at[0], across_h
        )
        swaps[w].start()
        started.append(swaps[w])

    def owner(g, t):
        return m * 8 + t // 2, (l if g == 0 else 1 - l) * 2 + lax.rem(t, 2)

    def itself(g, t):
        return jnp.logical_and(owner(g, t)[0] == dp, owner(g, t)[1] == m)

    def spot(g):
        return r["landed"].at[dp] if g == 0 else r["landed"].at[dp, g - 1]

    def outgoing(g, t):
        return remote(r[f"dense{g}"].at[t], spot(g), r[f"out_send{g}"].at[t], r[f"out_recv{g}"].at[dp], owner(g, t))

    def deliver(g):
        tiles, dense = r[f"tiles{g}"], r[f"dense{g}"]
        for w, (group, first, n) in enumerate(WAVES):
            if group == g:
                swaps[w].wait_recv()
                tiles[pl.ds(first, n)] = r[f"last{w}"][h] + r[f"over{w}"][...]
        tiles[GROUP_SLOTS[g]] = jnp.zeros((8, BLOCK), F32)

        def one(t, carry):
            core_to = lax.rem(t, 2)
            for lo in range(2):
                row = (t // 2) * 2 + lo
                if g == 0:
                    for cc in range(2):
                        dense[t, cc, lo] = tiles[table_ref[row, core_to * 2 + cc]]
                else:
                    dense[t, lo] = tiles[table_ref[row, FIRST_COL[g] + core_to]]

            @pl.when(itself(g, t))
            def _():
                pltpu.make_async_copy(dense.at[t], spot(g), r[f"out_recv{g}"].at[dp]).start()

            @pl.when(jnp.logical_not(itself(g, t)))
            def _():
                outgoing(g, t).start()

            return carry

        lax.fori_loop(0, 16, one, 0)

    def drain(g):
        def one(t, carry):
            @pl.when(jnp.logical_not(itself(g, t)))
            def _():
                outgoing(g, t).wait_send()

            return carry

        lax.fori_loop(0, 16, one, 0)

    def forward(cc):
        for i, (piece_cc, g) in enumerate(pieces):
            if piece_cc == cc:
                fars[i].wait_recv()
                place = r[f"cots{1 + cc}"].at[core, :, lanes(g)]
                copy = remote(place, place, r["fwd_send"].at[i], r["fwd_recv"].at[i], pair)
                copy.start()
                fwds.append(copy)

    def forwarded(cc):
        for copy in fwds[cc * 2 : cc * 2 + 2]:
            copy.wait_recv()

    for copy in inputs:
        copy.wait()
    for copy in pairs:
        copy.wait_recv()
    products(0)
    open_first(0)
    products(1)
    open_first(1)
    turn_first(0)
    forward(0)
    turn_first(1)
    forwarded(0)
    products(2)
    open_first(2)
    close_first(0)
    close_first(1)
    turn_first(2)
    forward(1)
    forwarded(1)
    products(3)
    open_first(3)
    turn_second(0)
    turn_second(1)
    close_second(0)
    close_second(1)
    close_first(2)
    turn_first(3)
    turn_second(2)
    deliver(0)
    close_second(2)
    close_first(3)
    deliver(1)
    turn_second(3)
    close_second(3)
    deliver(2)

    def arrived(g):
        def one(i, carry):
            place = r["landed"].at[i] if g == 0 else r["landed"].at[i, g - 1]
            pltpu.make_async_copy(place, place, r[f"out_recv{g}"].at[i]).wait()
            return carry

        lax.fori_loop(0, 32, one, 0)

    moment_in.wait()
    curvature_in.wait()

    @pl.when(m // 2 == x // 2)
    def _():
        arrived(0)

    @pl.when(m // 2 != x // 2)
    def _():
        arrived(1)
        arrived(2)

    def finish(strip, carry):
        from_true = strip * 2
        from_sampled = (lax.rem(strip, 4) * 4 + strip // 4) * 2 + 1
        for cc in range(2):
            for lo in range(2):
                at = (pl.ds(pl.multiple_of(lo * BLOCK + strip * 8, 8), 8), pl.ds(cc * BLOCK, BLOCK))
                sum_true = r["landed"][from_true, cc, lo] + sums_in[(0, *at)]
                sum_sampled = r["landed"][from_sampled, cc, lo] + sums_in[(1, *at)]
                sums_ref[(0, *at)] = sum_true
                sums_ref[(1, *at)] = sum_sampled
                grad_true = sum_true * (1.0 / tokens_all)
                grad_sampled = sum_sampled * (1.0 / tokens_all)
                moment_new = BETA_ONE * r["moment"][at] + (1.0 - BETA_ONE) * grad_true
                hessian = tokens_all * grad_sampled * grad_sampled
                curvature_next = BETA_TWO * r["curvature"][at] + (1.0 - BETA_TWO) * hessian
                update = jnp.clip(moment_new / (GAMMA_CLIP * curvature_next), -1.0, 1.0)
                kept = mask_ref[dp * 2 + lo, m * 2 + cc].astype(F32)
                update_ref[at] = update * kept
                new_curvature_ref[at] = curvature_next * kept
        return carry

    lax.fori_loop(0, 16, finish, 0)

    for copy in (*fars, *pairs, *fwds, *started):
        copy.wait_send()
    for g in range(3):
        drain(g)


def round_step(tokens_all, *args):
    vmem = pl.BlockSpec(memory_space=pltpu.VMEM)
    smem = pl.BlockSpec(memory_space=pltpu.SMEM)
    hbm = pl.BlockSpec(memory_space=pl.ANY)
    block = jax.ShapeDtypeStruct((2 * BLOCK, 2 * BLOCK), F32)
    return pl.pallas_call(
        functools.partial(kernel, tokens_all),
        out_shape=(block, block, jax.ShapeDtypeStruct((2, 2 * BLOCK, 2 * BLOCK), F32)),
        in_specs=[smem, smem, hbm, hbm, hbm, hbm, hbm, vmem],
        out_specs=(vmem,) * 3,
        scratch_shapes=list(scratch_list(args[2].shape[0]).values()),
        compiler_params=pltpu.CompilerParams(
            collective_id=0, has_side_effects=True, vmem_limit_bytes=60 << 20
        ),
        name="round_step",
    )(*args)


def table_kernel(round_ref, mask_ref, table_ref):
    m = lax.axis_index("mp")
    half = m // 2
    own = mask_ref[pl.ds(pl.multiple_of(m * TILE_ROWS, TILE_ROWS), TILE_ROWS), :]
    kept_all = jnp.where(own > 0, 1, 0)
    row_index = lax.broadcasted_iota(I32, (TILE_ROWS, 1), 0)
    slot_index = lax.broadcasted_iota(I32, (TILE_ROWS, BLOCK), 1)
    lane = lax.broadcasted_iota(I32, (TILE_ROWS, BLOCK), 1)
    before_rows = lax.broadcasted_iota(I32, (TILE_ROWS, TILE_ROWS), 1) < lax.broadcasted_iota(
        I32, (TILE_ROWS, TILE_ROWS), 0
    )
    place = jnp.zeros((TILE_ROWS, BLOCK), I32)
    lines = []
    for g, cols in enumerate(GROUP_COLS):
        n = GROUP_SLOTS[g]
        near, other = (
            [half_ * 4 + k for k in range(4)] if g == 0 else [(1 - half_) * 4 + k * 2 + g - 1 for k in range(2)]
            for half_ in range(2)
        )
        kept = [
            jnp.where(half == 0, kept_all[:, near[k] : near[k] + 1], kept_all[:, other[k] : other[k] + 1])
            for k in range(cols)
        ]
        per_row = functools.reduce(lambda p, q: p + q, kept)
        turned = jnp.sum(
            jnp.where(
                lax.broadcasted_iota(I32, (TILE_ROWS, TILE_ROWS), 0)
                == lax.broadcasted_iota(I32, (TILE_ROWS, TILE_ROWS), 1),
                per_row, 0,
            ),
            axis=0, keepdims=True,
        )
        seen = jnp.sum(jnp.where(before_rows, turned, 0), axis=1, keepdims=True) - round_ref[0] * n
        rows_line = jnp.zeros((1, BLOCK), I32)
        cols_line = jnp.zeros((1, BLOCK), I32)
        for k in range(cols):
            here = (kept[k] > 0) & (seen >= 0) & (seen < n)
            place = jnp.where(lane == FIRST_COL[g] + k, jnp.where(here, seen, n), place)
            chosen = jnp.where(here, seen, -1) == slot_index
            rows_line = rows_line + jnp.sum(jnp.where(chosen, row_index, 0), axis=0, keepdims=True)
            cols_line = cols_line + jnp.sum(jnp.where(chosen, k, 0), axis=0, keepdims=True)
            seen = seen + kept[k]
        lines += [rows_line, cols_line]

    counts = jnp.sum(jnp.where(mask_ref[...] > 0, 1, 0).reshape(4, TILE_ROWS, 8), axis=1)
    source = lax.broadcasted_iota(I32, (4, 8), 0)
    column = lax.broadcasted_iota(I32, (4, 8), 1)
    near = (source // 2) == (column // 4)
    even = lax.rem(column, 2) == 0
    needed = jnp.zeros((4, 1), I32)
    for g, inside in enumerate((near, ~near & even, ~near & ~even)):
        filled = jnp.sum(jnp.where(inside, counts, 0), axis=1, keepdims=True)
        rounds = sum(jnp.where(filled > n * GROUP_SLOTS[g], 1, 0) for n in range(TILE_ROWS * GROUP_COLS[g] // GROUP_SLOTS[g] + 1))
        needed = jnp.maximum(needed, rounds)
    lines.append(jnp.broadcast_to(jnp.max(needed, axis=0, keepdims=True), (1, BLOCK)))
    table_ref[pl.ds(0, TILE_ROWS)] = place
    for i, line in enumerate(lines):
        table_ref[pl.ds(TILE_ROWS + i, 1)] = line
    table_ref[pl.ds(TILE_ROWS + len(lines), 1)] = jnp.zeros((1, BLOCK), I32)


def table_of(tile_mask, round_):
    return pl.pallas_call(
        table_kernel,
        out_shape=jax.ShapeDtypeStruct(TABLE, I32),
        in_specs=[pl.BlockSpec(memory_space=pltpu.SMEM), pl.BlockSpec(memory_space=pltpu.VMEM)],
        out_specs=pl.BlockSpec(memory_space=pltpu.VMEM),
        name="tables",
    )(round_.reshape(1), tile_mask)


def on_device(activations, cot_true, cot_sampled, tile_mask, moment, curvature):
    tokens_all = activations.shape[0] * lax.axis_size("dp")

    def more(state):
        round_, rounds = state[:2]
        return round_ < rounds

    def step(state):
        round_, _, _, _, sums = state
        table = table_of(tile_mask, round_)
        update, new_curvature, sums = round_step(
            tokens_all, table, tile_mask, activations, cot_true, cot_sampled, moment, curvature, sums
        )
        return round_ + 1, table[ROUNDS_AT, 0], update, new_curvature, sums

    start = (jnp.int32(0), jnp.int32(1), moment, curvature, jnp.zeros((2, 2 * BLOCK, 2 * BLOCK), F32))
    _, _, update, new_curvature, _ = lax.while_loop(more, step, start)
    return update, new_curvature


def solution(mesh):
    return jax.shard_map(
        on_device,
        mesh=mesh,
        in_specs=(P("dp", "mp"), P("dp", "mp"), P("dp", "mp"), P(), P("dp", "mp"), P("dp", "mp")),
        out_specs=(P("dp", "mp"), P("dp", "mp")),
        check_vma=False,
    )
```

```python
import functools

import jax
import jax.numpy as jnp
from jax import lax
from jax.experimental import pallas as pl
from jax.experimental.pallas import tpu as pltpu
from jax.sharding import PartitionSpec as P

D = 8192
BLOCK = 128
BETA_ONE = 0.965
BETA_TWO = 0.99
GAMMA_CLIP = 0.01
MESH = pl.DeviceIdType.MESH
F32, BF16, I32 = jnp.float32, jnp.bfloat16, jnp.int32

GROUP_COLS = (4, 2, 2)
WAVES = ((0, 0, 14), (0, 14, 12), (1, 0, 16), (2, 0, 16))
GROUP_SLOTS = tuple(sum(n for g, _, n in WAVES if g == group) for group in range(3))
TILE_ROWS = 16

FIRST_COL = (0, 4, 6)
LIST_AT = TILE_ROWS
TABLE = (TILE_ROWS + 8, BLOCK)


def remote(src, dst, send_sem, recv_sem, device):
    return pltpu.make_async_remote_copy(
        src_ref=src, dst_ref=dst, send_sem=send_sem, recv_sem=recv_sem,
        device_id=device, device_id_type=MESH,
    )


def scratch_list(tokens):
    dma = pltpu.SemaphoreType.DMA
    shapes = dict(
        acts=pltpu.VMEM((tokens, TILE_ROWS * BLOCK), BF16),
        acts_t=pltpu.VMEM((TILE_ROWS, BLOCK, tokens), BF16),
        landed=pltpu.VMEM((32, 2, 2, 8, BLOCK), F32),
        in_sem=dma((5,)),
        pair_send=dma((4,)), pair_recv=dma((4,)),
        far_send=dma((4,)), far_recv=dma((4,)),
        fwd_send=dma((4,)), fwd_recv=dma((4,)),
    )
    for g, cols in enumerate(GROUP_COLS):
        n = GROUP_SLOTS[g]
        shapes[f"cots{g}"] = pltpu.VMEM((cols, tokens, 2 * BLOCK), BF16)
        shapes[f"tiles{g}"] = pltpu.VMEM((n + 1, 8, BLOCK), F32)
        per_owner = (2, 2) if g == 0 else (2,)
        shapes[f"dense{g}"] = pltpu.VMEM((16, *per_owner, 8, BLOCK), F32)
        shapes[f"out_send{g}"] = dma((16,))
        shapes[f"out_recv{g}"] = dma((32,))
    for w, (_, _, n) in enumerate(WAVES):
        half = n // 2
        shapes[f"part{w}"] = pltpu.VMEM((2, 16, n, 8, BLOCK), F32)
        shapes[f"relay1_{w}"] = pltpu.VMEM((2, 2, 2, n, 8, BLOCK), F32)
        shapes[f"final1_{w}"] = pltpu.VMEM((2, 4, 2, n, 8, BLOCK), F32)
        shapes[f"relay2_{w}"] = pltpu.VMEM((2, 2, half, 8, BLOCK), F32)
        shapes[f"final2_{w}"] = pltpu.VMEM((2, 4, half, 8, BLOCK), F32)
        shapes[f"mid{w}"] = pltpu.VMEM((2, 4, n, 8, BLOCK), F32)
        shapes[f"last{w}"] = pltpu.VMEM((2, n, 8, BLOCK), F32)
        shapes[f"over{w}"] = pltpu.VMEM((n, 8, BLOCK), F32)
        shapes[f"ring_send{w}"] = dma((2, 2, 6))
        shapes[f"ring_recv{w}"] = dma((2, 2, 6))
        shapes[f"swap_send{w}"] = dma((1,))
        shapes[f"swap_recv{w}"] = dma((1,))
    return shapes


def kernel(*refs):
    refs = list(refs)
    names = list(scratch_list(8))
    r = dict(zip(names, refs[-len(names):]))
    table_ref, acts_hbm, true_ref, sampled_ref, sums_ref = refs[: -len(names)]

    dp = lax.axis_index("dp")
    m = lax.axis_index("mp")
    x, z, h = dp // 8, lax.rem(dp // 2, 4), lax.rem(dp, 2)
    l, core = m // 2, lax.rem(m, 2)

    def device_at(x, z, h, m):
        return (x * 8 + z * 2 + h, m)

    pair = device_at(x, z, h, l * 2 + 1 - core)
    far = device_at(x, z, h, (1 - l) * 2 + core)
    along_x = [device_at(lax.rem(x + d, 4), z, h, m) for d in (1, 3)]
    along_z = [device_at(x, lax.rem(z + d, 4), h, m) for d in (1, 3)]
    across_h = device_at(x, z, 1 - h, m)

    acts_in = pltpu.make_async_copy(acts_hbm, r["acts"], r["in_sem"].at[0])
    acts_in.start()

    barrier = pltpu.get_barrier_semaphore()
    for other in (pair, far, *along_x, *along_z, across_h):
        pl.semaphore_signal(barrier, inc=1, device_id=other, device_id_type=MESH)

    def greet(sender, carry):
        @pl.when(jnp.logical_not(jnp.logical_and(sender == dp, m == x)))
        def _():
            pl.semaphore_signal(barrier, inc=1, device_id=(sender, x), device_id_type=MESH)
        return carry

    lax.fori_loop(0, 32, greet, 0)
    pl.semaphore_wait(barrier, jnp.where(m == x, 38, 39))

    def own(cc, g):
        return (true_ref, sampled_ref)[g].at[:, pl.ds(cc * BLOCK, BLOCK)]

    def lanes(g):
        return pl.ds(g * BLOCK, BLOCK)

    pieces = [(cc, g) for cc in range(2) for g in range(2)]
    inputs, pairs, fars, fwds, started = [], [], [], [], []
    for i, (cc, g) in enumerate(pieces):
        near_place = r["cots0"].at[core * 2 + cc, :, lanes(g)]
        far_place = r[f"cots{1 + cc}"].at[core, :, lanes(g)]
        fars.append(remote(own(cc, g), far_place, r["far_send"].at[i], r["far_recv"].at[i], far))
        pairs.append(remote(own(cc, g), near_place, r["pair_send"].at[i], r["pair_recv"].at[i], pair))
        inputs.append(pltpu.make_async_copy(own(cc, g), near_place, r["in_sem"].at[1 + i]))
    for copies in (fars, pairs, inputs):
        for copy in copies:
            copy.start()
    acts_in.wait()

    def transpose(row, carry):
        r["acts_t"][row] = r["acts"][:, pl.ds(pl.multiple_of(row * BLOCK, BLOCK), BLOCK)].T
        return carry

    lax.fori_loop(0, TILE_ROWS, transpose, 0)

    def products(w):
        group, first, n = WAVES[w]
        cots, part = r[f"cots{group}"], r[f"part{w}"]

        def one(i, carry):
            for u in range(2):
                s = 2 * i + u
                row = table_ref[LIST_AT + 2 * group, first + s]
                col = table_ref[LIST_AT + 2 * group + 1, first + s]
                tile = jnp.dot(r["acts_t"][row], cots[col], preferred_element_type=F32)
                for g in range(2):
                    part[g, :, s] = tile[:, g * BLOCK : (g + 1) * BLOCK].reshape(16, 8, BLOCK)
            return carry

        lax.fori_loop(0, n // 2, one, 0)

    def ring_open(send, recv, pos, neighbours, chunk, relay, final):
        up, down = neighbours
        nxt, opposite, prv = (lax.rem(pos + d, 4) for d in (1, 2, 3))
        copies = [
            remote(chunk(opposite, 0), relay.at[0], send.at[0], recv.at[0], up),
            remote(chunk(opposite, 1), relay.at[1], send.at[1], recv.at[1], down),
            remote(chunk(nxt, 1), final.at[0], send.at[2], recv.at[2], up),
            remote(chunk(prv, 0), final.at[1], send.at[3], recv.at[3], down),
            remote(relay.at[0], final.at[2], send.at[4], recv.at[4], up),
            remote(relay.at[1], final.at[3], send.at[5], recv.at[5], down),
        ]
        for copy in copies[:4]:
            copy.start()
        started.extend(copies)
        return copies

    def ring_turn(copies, pos, chunk, relay, add):
        for i, d in enumerate((1, 3)):
            copies[i].wait_recv()
            add(relay.at[i], (relay.at[i], chunk(lax.rem(pos + d, 4), i)))
            copies[4 + i].start()

    def ring_close(copies, pos, chunk, final, add, result):
        for copy in copies[2:]:
            copy.wait_recv()
        add(result(0), (chunk(pos, 0), final.at[1], final.at[2]))
        add(result(1), (chunk(pos, 1), final.at[0], final.at[3]))

    def add_big(dst, srcs):
        for i in range(2):
            total = srcs[0][i] + srcs[1][i]
            for src in srcs[2:]:
                total = total + src[i]
            dst[i] = total

    def add_small(dst, srcs):
        total = srcs[0][...] + srcs[1][...]
        for src in srcs[2:]:
            total = total + src[...]
        dst[...] = total

    streams = ((x, along_x, z, along_z), (z, along_z, x, along_x))
    first_ring, second_ring, swaps = {}, {}, {}

    def chunk1(w, s):
        return lambda p, half: r[f"part{w}"].at[s, pl.ds(p * 4 + half * 2, 2)]

    def chunk2(w, s):
        half_n = WAVES[w][2] // 2
        return lambda p, half: r[f"mid{w}"].at[s, p, pl.ds(half * half_n, half_n)]

    def open_first(w):
        for s, (pos, near, _, _) in enumerate(streams):
            first_ring[w, s] = ring_open(
                r[f"ring_send{w}"].at[s, 0], r[f"ring_recv{w}"].at[s, 0], pos, near, chunk1(w, s),
                r[f"relay1_{w}"].at[s], r[f"final1_{w}"].at[s],
            )

    def turn_first(w):
        for s, (pos, _, _, _) in enumerate(streams):
            ring_turn(first_ring[w, s], pos, chunk1(w, s), r[f"relay1_{w}"].at[s], add_big)

    def close_first(w):
        for s, (pos, _, pos2, near2) in enumerate(streams):
            ring_close(
                first_ring[w, s], pos, chunk1(w, s), r[f"final1_{w}"].at[s], add_big,
                lambda half: r[f"mid{w}"].at[s, pl.ds(half * 2, 2)],
            )
            second_ring[w, s] = ring_open(
                r[f"ring_send{w}"].at[s, 1], r[f"ring_recv{w}"].at[s, 1], pos2, near2, chunk2(w, s),
                r[f"relay2_{w}"].at[s], r[f"final2_{w}"].at[s],
            )

    def turn_second(w):
        for s, (_, _, pos2, _) in enumerate(streams):
            ring_turn(second_ring[w, s], pos2, chunk2(w, s), r[f"relay2_{w}"].at[s], add_small)

    def close_second(w):
        half_n = WAVES[w][2] // 2
        for s, (_, _, pos2, _) in enumerate(streams):
            ring_close(
                second_ring[w, s], pos2, chunk2(w, s), r[f"final2_{w}"].at[s], add_small,
                lambda half: r[f"last{w}"].at[s, pl.ds(half * half_n, half_n)],
            )
        swaps[w] = remote(
            r[f"last{w}"].at[1 - h], r[f"over{w}"], r[f"swap_send{w}"].at[0], r[f"swap_recv{w}"].at[0], across_h
        )
        swaps[w].start()
        started.append(swaps[w])

    def owner(g, t):
        return m * 8 + t // 2, (l if g == 0 else 1 - l) * 2 + lax.rem(t, 2)

    def itself(g, t):
        return jnp.logical_and(owner(g, t)[0] == dp, owner(g, t)[1] == m)

    def spot(g):
        return r["landed"].at[dp] if g == 0 else r["landed"].at[dp, g - 1]

    def outgoing(g, t):
        return remote(r[f"dense{g}"].at[t], spot(g), r[f"out_send{g}"].at[t], r[f"out_recv{g}"].at[dp], owner(g, t))

    def deliver(g):
        tiles, dense = r[f"tiles{g}"], r[f"dense{g}"]
        for w, (group, first, n) in enumerate(WAVES):
            if group == g:
                swaps[w].wait_recv()
                tiles[pl.ds(first, n)] = r[f"last{w}"][h] + r[f"over{w}"][...]
        tiles[GROUP_SLOTS[g]] = jnp.zeros((8, BLOCK), F32)

        def one(t, carry):
            core_to = lax.rem(t, 2)
            for lo in range(2):
                row = (t // 2) * 2 + lo
                if g == 0:
                    for cc in range(2):
                        dense[t, cc, lo] = tiles[table_ref[row, core_to * 2 + cc]]
                else:
                    dense[t, lo] = tiles[table_ref[row, FIRST_COL[g] + core_to]]

            @pl.when(itself(g, t))
            def _():
                pltpu.make_async_copy(dense.at[t], spot(g), r[f"out_recv{g}"].at[dp]).start()

            @pl.when(jnp.logical_not(itself(g, t)))
            def _():
                outgoing(g, t).start()

            return carry

        lax.fori_loop(0, 16, one, 0)

    def drain(g):
        def one(t, carry):
            @pl.when(jnp.logical_not(itself(g, t)))
            def _():
                outgoing(g, t).wait_send()

            return carry

        lax.fori_loop(0, 16, one, 0)

    def forward(cc):
        for i, (piece_cc, g) in enumerate(pieces):
            if piece_cc == cc:
                fars[i].wait_recv()
                place = r[f"cots{1 + cc}"].at[core, :, lanes(g)]
                copy = remote(place, place, r["fwd_send"].at[i], r["fwd_recv"].at[i], pair)
                copy.start()
                fwds.append(copy)

    def forwarded(cc):
        for copy in fwds[cc * 2 : cc * 2 + 2]:
            copy.wait_recv()

    for copy in inputs:
        copy.wait()
    for copy in pairs:
        copy.wait_recv()
    products(0)
    open_first(0)
    products(1)
    open_first(1)
    turn_first(0)
    forward(0)
    turn_first(1)
    forwarded(0)
    products(2)
    open_first(2)
    close_first(0)
    close_first(1)
    turn_first(2)
    forward(1)
    forwarded(1)
    products(3)
    open_first(3)
    turn_second(0)
    turn_second(1)
    close_second(0)
    close_second(1)
    close_first(2)
    turn_first(3)
    turn_second(2)
    deliver(0)
    close_second(2)
    close_first(3)
    deliver(1)
    turn_second(3)
    close_second(3)
    deliver(2)

    def arrived(g):
        def one(i, carry):
            place = r["landed"].at[i] if g == 0 else r["landed"].at[i, g - 1]
            pltpu.make_async_copy(place, place, r[f"out_recv{g}"].at[i]).wait()
            return carry

        lax.fori_loop(0, 32, one, 0)

    @pl.when(m // 2 == x // 2)
    def _():
        arrived(0)

    @pl.when(m // 2 != x // 2)
    def _():
        arrived(1)
        arrived(2)

    def finish(strip, carry):
        from_true = strip * 2
        from_sampled = (lax.rem(strip, 4) * 4 + strip // 4) * 2 + 1
        for cc in range(2):
            for lo in range(2):
                at = (pl.ds(pl.multiple_of(lo * BLOCK + strip * 8, 8), 8), pl.ds(cc * BLOCK, BLOCK))
                sums_ref[(0, *at)] = r["landed"][from_true, cc, lo]
                sums_ref[(1, *at)] = r["landed"][from_sampled, cc, lo]
        return carry

    lax.fori_loop(0, 16, finish, 0)

    for copy in (*fars, *pairs, *fwds, *started):
        copy.wait_send()
    for g in range(3):
        drain(g)


def round_step(*args):
    smem = pl.BlockSpec(memory_space=pltpu.SMEM)
    hbm = pl.BlockSpec(memory_space=pl.ANY)
    return pl.pallas_call(
        kernel,
        out_shape=jax.ShapeDtypeStruct((2, 2 * BLOCK, 2 * BLOCK), F32),
        in_specs=[smem, hbm, hbm, hbm],
        out_specs=pl.BlockSpec(memory_space=pltpu.VMEM),
        scratch_shapes=list(scratch_list(args[1].shape[0]).values()),
        compiler_params=pltpu.CompilerParams(
            collective_id=0, has_side_effects=True, vmem_limit_bytes=60 << 20
        ),
        name="round_step",
    )(*args)


def table_kernel(round_ref, mask_ref, table_ref, rounds_ref):
    m = lax.axis_index("mp")
    half = m // 2
    own = mask_ref[pl.ds(pl.multiple_of(m * TILE_ROWS, TILE_ROWS), TILE_ROWS), :]
    kept_all = jnp.where(own > 0, 1, 0)
    row_index = lax.broadcasted_iota(I32, (TILE_ROWS, 1), 0)
    slot_index = lax.broadcasted_iota(I32, (TILE_ROWS, BLOCK), 1)
    lane = lax.broadcasted_iota(I32, (TILE_ROWS, BLOCK), 1)
    before_rows = lax.broadcasted_iota(I32, (TILE_ROWS, TILE_ROWS), 1) < lax.broadcasted_iota(
        I32, (TILE_ROWS, TILE_ROWS), 0
    )
    place = jnp.zeros((TILE_ROWS, BLOCK), I32)
    lines = []
    for g, cols in enumerate(GROUP_COLS):
        n = GROUP_SLOTS[g]
        near, other = (
            [half_ * 4 + k for k in range(4)] if g == 0 else [(1 - half_) * 4 + k * 2 + g - 1 for k in range(2)]
            for half_ in range(2)
        )
        kept = [
            jnp.where(half == 0, kept_all[:, near[k] : near[k] + 1], kept_all[:, other[k] : other[k] + 1])
            for k in range(cols)
        ]
        per_row = functools.reduce(lambda p, q: p + q, kept)
        turned = jnp.sum(
            jnp.where(
                lax.broadcasted_iota(I32, (TILE_ROWS, TILE_ROWS), 0)
                == lax.broadcasted_iota(I32, (TILE_ROWS, TILE_ROWS), 1),
                per_row, 0,
            ),
            axis=0, keepdims=True,
        )
        seen = jnp.sum(jnp.where(before_rows, turned, 0), axis=1, keepdims=True) - round_ref[0] * n
        rows_line = jnp.zeros((1, BLOCK), I32)
        cols_line = jnp.zeros((1, BLOCK), I32)
        for k in range(cols):
            here = (kept[k] > 0) & (seen >= 0) & (seen < n)
            place = jnp.where(lane == FIRST_COL[g] + k, jnp.where(here, seen, n), place)
            chosen = jnp.where(here, seen, -1) == slot_index
            rows_line = rows_line + jnp.sum(jnp.where(chosen, row_index, 0), axis=0, keepdims=True)
            cols_line = cols_line + jnp.sum(jnp.where(chosen, k, 0), axis=0, keepdims=True)
            seen = seen + kept[k]
        lines += [rows_line, cols_line]

    counts = jnp.sum(jnp.where(mask_ref[...] > 0, 1, 0).reshape(4, TILE_ROWS, 8), axis=1)
    source = lax.broadcasted_iota(I32, (4, 8), 0)
    column = lax.broadcasted_iota(I32, (4, 8), 1)
    near = (source // 2) == (column // 4)
    even = lax.rem(column, 2) == 0
    needed = jnp.zeros((4, 1), I32)
    for g, inside in enumerate((near, ~near & even, ~near & ~even)):
        filled = jnp.sum(jnp.where(inside, counts, 0), axis=1, keepdims=True)
        rounds = sum(jnp.where(filled > n * GROUP_SLOTS[g], 1, 0) for n in range(TILE_ROWS * GROUP_COLS[g] // GROUP_SLOTS[g] + 1))
        needed = jnp.maximum(needed, rounds)
    rounds_ref[0] = jnp.max(needed)
    lines.append(jnp.zeros((2, BLOCK), I32))
    table_ref[pl.ds(0, TILE_ROWS)] = place
    table_ref[pl.ds(TILE_ROWS, 8)] = jnp.concatenate(lines, axis=0)


def table_of(tile_mask, round_):
    return pl.pallas_call(
        table_kernel,
        out_shape=(jax.ShapeDtypeStruct(TABLE, I32), jax.ShapeDtypeStruct((1,), I32)),
        in_specs=[pl.BlockSpec(memory_space=pltpu.SMEM), pl.BlockSpec(memory_space=pltpu.VMEM)],
        out_specs=(pl.BlockSpec(memory_space=pltpu.VMEM), pl.BlockSpec(memory_space=pltpu.SMEM)),
        name="tables",
    )(round_.reshape(1), tile_mask)


def on_device(activations, cot_true, cot_sampled, tile_mask, moment, curvature):
    m = lax.axis_index("mp")
    dp = lax.axis_index("dp")
    tokens_all = activations.shape[0] * lax.axis_size("dp")

    def one_round(round_):
        table, rounds = table_of(tile_mask, round_)
        return round_step(table, activations, cot_true, cot_sampled), rounds

    sums, rounds = one_round(jnp.int32(0))
    _, sums = lax.while_loop(
        lambda state: state[0] < rounds[0],
        lambda state: (state[0] + 1, state[1] + one_round(state[0])[0]),
        (jnp.int32(1), sums),
    )
    owned = lax.dynamic_slice(tile_mask, (dp * 2, m * 2), (2, 2))
    owned_mask = jnp.repeat(jnp.repeat(owned, BLOCK, axis=0), BLOCK, axis=1).astype(F32)
    grads = sums * (1.0 / tokens_all)
    moment_new = BETA_ONE * moment + (1.0 - BETA_ONE) * grads[0]
    hessian = tokens_all * grads[1] * grads[1]
    curvature_next = BETA_TWO * curvature + (1.0 - BETA_TWO) * hessian
    update = jnp.clip(moment_new / (GAMMA_CLIP * curvature_next), -1.0, 1.0) * owned_mask
    return update, curvature_next * owned_mask


def solution(mesh):
    return jax.shard_map(
        on_device,
        mesh=mesh,
        in_specs=(P("dp", "mp"), P("dp", "mp"), P("dp", "mp"), P(), P("dp", "mp"), P("dp", "mp")),
        out_specs=(P("dp", "mp"), P("dp", "mp")),
        check_vma=False,
    )
```

```python
import functools

import jax
import jax.numpy as jnp
from jax import lax
from jax.experimental import pallas as pl
from jax.experimental.pallas import tpu as pltpu
from jax.sharding import PartitionSpec as P

D = 8192
BLOCK = 128
BETA_ONE = 0.965
BETA_TWO = 0.99
GAMMA_CLIP = 0.01
MESH = pl.DeviceIdType.MESH
F32, BF16, I32 = jnp.float32, jnp.bfloat16, jnp.int32

GROUP_COLS = (4, 2, 2)
WAVES = ((0, 0, 14), (0, 14, 12), (1, 0, 16), (2, 0, 16))
GROUP_SLOTS = tuple(sum(n for g, _, n in WAVES if g == group) for group in range(3))
TILE_ROWS = 16
CHUNKS = (((0, 8),), ((0, 8),), ((0, 4), (4, 2), (6, 2)))
FAR_PIECES = tuple((cc, c, g) for cc in range(2) for c in range(len(CHUNKS[1 + cc])) for g in range(2))
NO_TILE = 3e38

FIRST_COL = (0, 4, 6)
LIST_AT = TILE_ROWS
TABLE = (TILE_ROWS + 8, BLOCK)


def remote(src, dst, send_sem, recv_sem, device):
    return pltpu.make_async_remote_copy(
        src_ref=src, dst_ref=dst, send_sem=send_sem, recv_sem=recv_sem,
        device_id=device, device_id_type=MESH,
    )


def scratch_list(tokens):
    dma = pltpu.SemaphoreType.DMA
    shapes = dict(
        acts=pltpu.VMEM((tokens, TILE_ROWS * BLOCK), BF16),
        acts_t=pltpu.VMEM((TILE_ROWS, BLOCK, tokens), BF16),
        landed=pltpu.VMEM((32, 2, 2, 8, BLOCK), F32),
        in_sem=dma((5,)),
        pair_send=dma((4,)), pair_recv=dma((4,)),
        far_send=dma((len(FAR_PIECES),)), far_recv=dma((len(FAR_PIECES),)),
        fwd_send=dma((len(FAR_PIECES),)), fwd_recv=dma((len(FAR_PIECES),)),
    )
    for g, cols in enumerate(GROUP_COLS):
        n = GROUP_SLOTS[g]
        for c, (_, eighths) in enumerate(CHUNKS[g]):
            shapes[f"cots{g}_{c}"] = pltpu.VMEM((cols, eighths * tokens // 8, 2 * BLOCK), BF16)
        shapes[f"tiles{g}"] = pltpu.VMEM((n + 1, 8, BLOCK), F32)
        per_owner = (2, 2) if g == 0 else (2,)
        shapes[f"dense{g}"] = pltpu.VMEM((16, *per_owner, 8, BLOCK), F32)
        shapes[f"out_send{g}"] = dma((16,))
        shapes[f"out_recv{g}"] = dma((32,))
    for w, (_, _, n) in enumerate(WAVES):
        half = n // 2
        shapes[f"part{w}"] = pltpu.VMEM((2, 16, n, 8, BLOCK), F32)
        shapes[f"relay1_{w}"] = pltpu.VMEM((2, 2, 2, n, 8, BLOCK), F32)
        shapes[f"final1_{w}"] = pltpu.VMEM((2, 4, 2, n, 8, BLOCK), F32)
        shapes[f"relay2_{w}"] = pltpu.VMEM((2, 2, half, 8, BLOCK), F32)
        shapes[f"final2_{w}"] = pltpu.VMEM((2, 4, half, 8, BLOCK), F32)
        shapes[f"mid{w}"] = pltpu.VMEM((2, 4, n, 8, BLOCK), F32)
        shapes[f"last{w}"] = pltpu.VMEM((2, n, 8, BLOCK), F32)
        shapes[f"over{w}"] = pltpu.VMEM((n, 8, BLOCK), F32)
        shapes[f"ring_send{w}"] = dma((2, 2, 6))
        shapes[f"ring_recv{w}"] = dma((2, 2, 6))
        shapes[f"swap_send{w}"] = dma((1,))
        shapes[f"swap_recv{w}"] = dma((1,))
    return shapes


def kernel(*refs):
    refs = list(refs)
    names = list(scratch_list(8))
    r = dict(zip(names, refs[-len(names):]))
    table_ref, acts_hbm, true_ref, sampled_ref, sums_ref = refs[: -len(names)]

    dp = lax.axis_index("dp")
    m = lax.axis_index("mp")
    x, z, h = dp // 8, lax.rem(dp // 2, 4), lax.rem(dp, 2)
    l, core = m // 2, lax.rem(m, 2)

    def device_at(x, z, h, m):
        return (x * 8 + z * 2 + h, m)

    pair = device_at(x, z, h, l * 2 + 1 - core)
    far = device_at(x, z, h, (1 - l) * 2 + core)
    along_x = [device_at(lax.rem(x + d, 4), z, h, m) for d in (1, 3)]
    along_z = [device_at(x, lax.rem(z + d, 4), h, m) for d in (1, 3)]
    across_h = device_at(x, z, 1 - h, m)

    acts_in = pltpu.make_async_copy(acts_hbm, r["acts"], r["in_sem"].at[0])
    acts_in.start()

    barrier = pltpu.get_barrier_semaphore()
    for other in (pair, far, *along_x, *along_z, across_h):
        pl.semaphore_signal(barrier, inc=1, device_id=other, device_id_type=MESH)

    def greet(sender, carry):
        @pl.when(jnp.logical_not(jnp.logical_and(sender == dp, m == x)))
        def _():
            pl.semaphore_signal(barrier, inc=1, device_id=(sender, x), device_id_type=MESH)
        return carry

    lax.fori_loop(0, 32, greet, 0)
    pl.semaphore_wait(barrier, jnp.where(m == x, 38, 39))

    eighth = true_ref.shape[0] // 8

    def own(cc, g, first=0, count=8):
        return (true_ref, sampled_ref)[g].at[pl.ds(first * eighth, count * eighth), lanes(cc)]

    def lanes(g):
        return pl.ds(g * BLOCK, BLOCK)

    def far_place(cc, c, g):
        return r[f"cots{1 + cc}_{c}"].at[core, :, lanes(g)]

    inputs, pairs, fars, fwds, started = [], [], [], {}, []
    for i, (cc, c, g) in enumerate(FAR_PIECES):
        piece = own(cc, g, *CHUNKS[1 + cc][c])
        fars.append(remote(piece, far_place(cc, c, g), r["far_send"].at[i], r["far_recv"].at[i], far))
    for i, (cc, g) in enumerate((cc, g) for cc in range(2) for g in range(2)):
        near_place = r["cots0_0"].at[core * 2 + cc, :, lanes(g)]
        pairs.append(remote(own(cc, g), near_place, r["pair_send"].at[i], r["pair_recv"].at[i], pair))
        inputs.append(pltpu.make_async_copy(own(cc, g), near_place, r["in_sem"].at[1 + i]))
    for copies in (fars, pairs, inputs):
        for copy in copies:
            copy.start()
    acts_in.wait()

    def transpose(row, carry):
        r["acts_t"][row] = r["acts"][:, pl.ds(pl.multiple_of(row * BLOCK, BLOCK), BLOCK)].T
        return carry

    lax.fori_loop(0, TILE_ROWS, transpose, 0)

    def products(w, c=0):
        group, first, n = WAVES[w]
        cots, part = r[f"cots{group}_{c}"], r[f"part{w}"]
        start, count = CHUNKS[group][c]

        def one(i, carry):
            for u in range(2):
                s = 2 * i + u
                row = table_ref[LIST_AT + 2 * group, first + s]
                col = table_ref[LIST_AT + 2 * group + 1, first + s]
                strip = r["acts_t"][row][:, start * eighth : (start + count) * eighth]
                tile = jnp.dot(strip, cots[col], preferred_element_type=F32)
                for g in range(2):
                    term = tile[:, g * BLOCK : (g + 1) * BLOCK].reshape(16, 8, BLOCK)
                    part[g, :, s] = term if c == 0 else part[g, :, s] + term
            return carry

        lax.fori_loop(0, n // 2, one, 0)

    def ring_open(send, recv, pos, neighbours, chunk, relay, final):
        up, down = neighbours
        nxt, opposite, prv = (lax.rem(pos + d, 4) for d in (1, 2, 3))
        copies = [
            remote(chunk(opposite, 0), relay.at[0], send.at[0], recv.at[0], up),
            remote(chunk(opposite, 1), relay.at[1], send.at[1], recv.at[1], down),
            remote(chunk(nxt, 1), final.at[0], send.at[2], recv.at[2], up),
            remote(chunk(prv, 0), final.at[1], send.at[3], recv.at[3], down),
            remote(relay.at[0], final.at[2], send.at[4], recv.at[4], up),
            remote(relay.at[1], final.at[3], send.at[5], recv.at[5], down),
        ]
        for copy in copies[:4]:
            copy.start()
        started.extend(copies)
        return copies

    def ring_turn(copies, pos, chunk, relay, add):
        for i, d in enumerate((1, 3)):
            copies[i].wait_recv()
            add(relay.at[i], (relay.at[i], chunk(lax.rem(pos + d, 4), i)))
            copies[4 + i].start()

    def ring_close(copies, pos, chunk, final, add, result):
        for copy in copies[2:]:
            copy.wait_recv()
        add(result(0), (chunk(pos, 0), final.at[1], final.at[2]))
        add(result(1), (chunk(pos, 1), final.at[0], final.at[3]))

    def add_big(dst, srcs):
        for i in range(2):
            total = srcs[0][i] + srcs[1][i]
            for src in srcs[2:]:
                total = total + src[i]
            dst[i] = total

    def add_small(dst, srcs):
        total = srcs[0][...] + srcs[1][...]
        for src in srcs[2:]:
            total = total + src[...]
        dst[...] = total

    streams = ((x, along_x, z, along_z), (z, along_z, x, along_x))
    first_ring, second_ring, swaps = {}, {}, {}

    def chunk1(w, s):
        return lambda p, half: r[f"part{w}"].at[s, pl.ds(p * 4 + half * 2, 2)]

    def chunk2(w, s):
        half_n = WAVES[w][2] // 2
        return lambda p, half: r[f"mid{w}"].at[s, p, pl.ds(half * half_n, half_n)]

    def open_first(w):
        for s, (pos, near, _, _) in enumerate(streams):
            first_ring[w, s] = ring_open(
                r[f"ring_send{w}"].at[s, 0], r[f"ring_recv{w}"].at[s, 0], pos, near, chunk1(w, s),
                r[f"relay1_{w}"].at[s], r[f"final1_{w}"].at[s],
            )

    def turn_first(w):
        for s, (pos, _, _, _) in enumerate(streams):
            ring_turn(first_ring[w, s], pos, chunk1(w, s), r[f"relay1_{w}"].at[s], add_big)

    def close_first(w):
        for s, (pos, _, pos2, near2) in enumerate(streams):
            ring_close(
                first_ring[w, s], pos, chunk1(w, s), r[f"final1_{w}"].at[s], add_big,
                lambda half: r[f"mid{w}"].at[s, pl.ds(half * 2, 2)],
            )
            second_ring[w, s] = ring_open(
                r[f"ring_send{w}"].at[s, 1], r[f"ring_recv{w}"].at[s, 1], pos2, near2, chunk2(w, s),
                r[f"relay2_{w}"].at[s], r[f"final2_{w}"].at[s],
            )

    def turn_second(w):
        for s, (_, _, pos2, _) in enumerate(streams):
            ring_turn(second_ring[w, s], pos2, chunk2(w, s), r[f"relay2_{w}"].at[s], add_small)

    def close_second(w):
        half_n = WAVES[w][2] // 2
        for s, (_, _, pos2, _) in enumerate(streams):
            ring_close(
                second_ring[w, s], pos2, chunk2(w, s), r[f"final2_{w}"].at[s], add_small,
                lambda half: r[f"last{w}"].at[s, pl.ds(half * half_n, half_n)],
            )
        swaps[w] = remote(
            r[f"last{w}"].at[1 - h], r[f"over{w}"], r[f"swap_send{w}"].at[0], r[f"swap_recv{w}"].at[0], across_h
        )
        swaps[w].start()
        started.append(swaps[w])

    def owner(g, t):
        return m * 8 + t // 2, (l if g == 0 else 1 - l) * 2 + lax.rem(t, 2)

    def itself(g, t):
        return jnp.logical_and(owner(g, t)[0] == dp, owner(g, t)[1] == m)

    def spot(g):
        return r["landed"].at[dp] if g == 0 else r["landed"].at[dp, g - 1]

    def outgoing(g, t):
        return remote(r[f"dense{g}"].at[t], spot(g), r[f"out_send{g}"].at[t], r[f"out_recv{g}"].at[dp], owner(g, t))

    def deliver(g):
        tiles, dense = r[f"tiles{g}"], r[f"dense{g}"]
        for w, (group, first, n) in enumerate(WAVES):
            if group == g:
                swaps[w].wait_recv()
                tiles[pl.ds(first, n)] = r[f"last{w}"][h] + r[f"over{w}"][...]
        tiles[GROUP_SLOTS[g]] = jnp.full((8, BLOCK), NO_TILE, F32)

        def one(t, carry):
            core_to = lax.rem(t, 2)
            for lo in range(2):
                row = (t // 2) * 2 + lo
                if g == 0:
                    for cc in range(2):
                        dense[t, cc, lo] = tiles[table_ref[row, core_to * 2 + cc]]
                else:
                    dense[t, lo] = tiles[table_ref[row, FIRST_COL[g] + core_to]]

            @pl.when(itself(g, t))
            def _():
                pltpu.make_async_copy(dense.at[t], spot(g), r[f"out_recv{g}"].at[dp]).start()

            @pl.when(jnp.logical_not(itself(g, t)))
            def _():
                outgoing(g, t).start()

            return carry

        lax.fori_loop(0, 16, one, 0)

    def drain(g):
        def one(t, carry):
            @pl.when(jnp.logical_not(itself(g, t)))
            def _():
                outgoing(g, t).wait_send()

            return carry

        lax.fori_loop(0, 16, one, 0)

    def forward(cc, c=0):
        for i, piece in enumerate(FAR_PIECES):
            if piece[:2] == (cc, c):
                fars[i].wait_recv()
                place = far_place(*piece)
                fwds[piece] = remote(place, place, r["fwd_send"].at[i], r["fwd_recv"].at[i], pair)
                fwds[piece].start()

    def forwarded(cc, c=0):
        for piece in FAR_PIECES:
            if piece[:2] == (cc, c):
                fwds[piece].wait_recv()

    for copy in inputs:
        copy.wait()
    for copy in pairs:
        copy.wait_recv()
    products(0)
    open_first(0)
    products(1)
    open_first(1)
    turn_first(0)
    forward(0)
    turn_first(1)
    forwarded(0)
    products(2)
    open_first(2)
    close_first(0)
    forward(1, 0)
    close_first(1)
    forwarded(1, 0)
    products(3, 0)
    forward(1, 1)
    forwarded(1, 1)
    products(3, 1)
    turn_first(2)
    forward(1, 2)
    forwarded(1, 2)
    products(3, 2)
    open_first(3)
    turn_second(0)
    turn_second(1)
    close_second(0)
    close_second(1)
    close_first(2)
    turn_first(3)
    turn_second(2)
    close_second(2)
    close_first(3)
    turn_second(3)
    deliver(0)
    deliver(1)
    close_second(3)
    deliver(2)

    def arrived(g):
        def one(i, carry):
            place = r["landed"].at[i] if g == 0 else r["landed"].at[i, g - 1]
            pltpu.make_async_copy(place, place, r[f"out_recv{g}"].at[i]).wait()
            return carry

        lax.fori_loop(0, 32, one, 0)

    @pl.when(m // 2 == x // 2)
    def _():
        arrived(0)

    @pl.when(m // 2 != x // 2)
    def _():
        arrived(1)
        arrived(2)

    def finish(strip, carry):
        from_true = strip * 2
        from_sampled = (lax.rem(strip, 4) * 4 + strip // 4) * 2 + 1
        for cc in range(2):
            for lo in range(2):
                at = (pl.ds(pl.multiple_of(lo * BLOCK + strip * 8, 8), 8), pl.ds(cc * BLOCK, BLOCK))
                sums_ref[(0, *at)] = r["landed"][from_true, cc, lo]
                sums_ref[(1, *at)] = r["landed"][from_sampled, cc, lo]
        return carry

    lax.fori_loop(0, 16, finish, 0)

    for copy in (*fars, *pairs, *fwds.values(), *started):
        copy.wait_send()
    for g in range(3):
        drain(g)


def round_step(*args):
    smem = pl.BlockSpec(memory_space=pltpu.SMEM)
    hbm = pl.BlockSpec(memory_space=pl.ANY)
    return pl.pallas_call(
        kernel,
        out_shape=jax.ShapeDtypeStruct((2, 2 * BLOCK, 2 * BLOCK), F32),
        in_specs=[smem, hbm, hbm, hbm],
        out_specs=pl.BlockSpec(memory_space=pltpu.VMEM),
        scratch_shapes=list(scratch_list(args[1].shape[0]).values()),
        compiler_params=pltpu.CompilerParams(
            collective_id=0, has_side_effects=True, vmem_limit_bytes=60 << 20
        ),
        name="round_step",
    )(*args)


def table_kernel(round_ref, mask_ref, table_ref, rounds_ref):
    m = lax.axis_index("mp")
    half = m // 2
    own = mask_ref[pl.ds(pl.multiple_of(m * TILE_ROWS, TILE_ROWS), TILE_ROWS), :]
    kept_all = jnp.where(own > 0, 1, 0)
    row_index = lax.broadcasted_iota(I32, (TILE_ROWS, 1), 0)
    slot_index = lax.broadcasted_iota(I32, (TILE_ROWS, BLOCK), 1)
    lane = lax.broadcasted_iota(I32, (TILE_ROWS, BLOCK), 1)
    before_rows = lax.broadcasted_iota(I32, (TILE_ROWS, TILE_ROWS), 1) < lax.broadcasted_iota(
        I32, (TILE_ROWS, TILE_ROWS), 0
    )
    place = jnp.zeros((TILE_ROWS, BLOCK), I32)
    lines = []
    for g, cols in enumerate(GROUP_COLS):
        n = GROUP_SLOTS[g]
        near, other = (
            [half_ * 4 + k for k in range(4)] if g == 0 else [(1 - half_) * 4 + k * 2 + g - 1 for k in range(2)]
            for half_ in range(2)
        )
        kept = [
            jnp.where(half == 0, kept_all[:, near[k] : near[k] + 1], kept_all[:, other[k] : other[k] + 1])
            for k in range(cols)
        ]
        per_row = functools.reduce(lambda p, q: p + q, kept)
        turned = jnp.sum(
            jnp.where(
                lax.broadcasted_iota(I32, (TILE_ROWS, TILE_ROWS), 0)
                == lax.broadcasted_iota(I32, (TILE_ROWS, TILE_ROWS), 1),
                per_row, 0,
            ),
            axis=0, keepdims=True,
        )
        seen = jnp.sum(jnp.where(before_rows, turned, 0), axis=1, keepdims=True) - round_ref[0] * n
        rows_line = jnp.zeros((1, BLOCK), I32)
        cols_line = jnp.zeros((1, BLOCK), I32)
        for k in range(cols):
            here = (kept[k] > 0) & (seen >= 0) & (seen < n)
            place = jnp.where(lane == FIRST_COL[g] + k, jnp.where(here, seen, n), place)
            chosen = jnp.where(here, seen, -1) == slot_index
            rows_line = rows_line + jnp.sum(jnp.where(chosen, row_index, 0), axis=0, keepdims=True)
            cols_line = cols_line + jnp.sum(jnp.where(chosen, k, 0), axis=0, keepdims=True)
            seen = seen + kept[k]
        lines += [rows_line, cols_line]

    counts = jnp.sum(jnp.where(mask_ref[...] > 0, 1, 0).reshape(4, TILE_ROWS, 8), axis=1)
    source = lax.broadcasted_iota(I32, (4, 8), 0)
    column = lax.broadcasted_iota(I32, (4, 8), 1)
    near = (source // 2) == (column // 4)
    even = lax.rem(column, 2) == 0
    needed = jnp.zeros((4, 1), I32)
    for g, inside in enumerate((near, ~near & even, ~near & ~even)):
        filled = jnp.sum(jnp.where(inside, counts, 0), axis=1, keepdims=True)
        rounds = sum(jnp.where(filled > n * GROUP_SLOTS[g], 1, 0) for n in range(TILE_ROWS * GROUP_COLS[g] // GROUP_SLOTS[g] + 1))
        needed = jnp.maximum(needed, rounds)
    rounds_ref[0] = jnp.max(needed)
    lines.append(jnp.zeros((2, BLOCK), I32))
    table_ref[pl.ds(0, TILE_ROWS)] = place
    table_ref[pl.ds(TILE_ROWS, 8)] = jnp.concatenate(lines, axis=0)


def table_of(tile_mask, round_):
    return pl.pallas_call(
        table_kernel,
        out_shape=(jax.ShapeDtypeStruct(TABLE, I32), jax.ShapeDtypeStruct((1,), I32)),
        in_specs=[pl.BlockSpec(memory_space=pltpu.SMEM), pl.BlockSpec(memory_space=pltpu.VMEM)],
        out_specs=(pl.BlockSpec(memory_space=pltpu.VMEM), pl.BlockSpec(memory_space=pltpu.SMEM)),
        name="tables",
    )(round_.reshape(1), tile_mask)


def on_device(activations, cot_true, cot_sampled, tile_mask, moment, curvature):
    tokens_all = activations.shape[0] * lax.axis_size("dp")

    def one_round(round_):
        table, rounds = table_of(tile_mask, round_)
        return round_step(table, activations, cot_true, cot_sampled), rounds

    sums, rounds = one_round(jnp.int32(0))
    def again(state):
        found, _ = one_round(state[0])
        return state[0] + 1, jnp.where(found < NO_TILE / 2, found, state[1])

    _, sums = lax.while_loop(lambda state: state[0] < rounds[0], again, (jnp.int32(1), sums))
    kept = sums[0] < NO_TILE / 2
    grads = sums * (1.0 / tokens_all)
    moment_new = BETA_ONE * moment + (1.0 - BETA_ONE) * grads[0]
    hessian = tokens_all * grads[1] * grads[1]
    curvature_next = BETA_TWO * curvature + (1.0 - BETA_TWO) * hessian
    update = jnp.clip(moment_new / (GAMMA_CLIP * curvature_next), -1.0, 1.0)
    return jnp.where(kept, update, 0.0), jnp.where(kept, curvature_next, 0.0)


def solution(mesh):
    return jax.shard_map(
        on_device,
        mesh=mesh,
        in_specs=(P("dp", "mp"), P("dp", "mp"), P("dp", "mp"), P(), P("dp", "mp"), P("dp", "mp")),
        out_specs=(P("dp", "mp"), P("dp", "mp")),
        check_vma=False,
    )
```

```python
import functools

import jax
import jax.numpy as jnp
from jax import lax
from jax.experimental import pallas as pl
from jax.experimental.pallas import tpu as pltpu
from jax.sharding import PartitionSpec as P

D = 8192
BLOCK = 128
BETA_ONE = 0.965
BETA_TWO = 0.99
GAMMA_CLIP = 0.01
MESH = pl.DeviceIdType.MESH
F32, BF16, I32 = jnp.float32, jnp.bfloat16, jnp.int32

GROUP_COLS = (4, 2, 2)
WAVES = ((0, 0, 14), (0, 14, 12), (1, 0, 16), (2, 0, 16))
GROUP_SLOTS = tuple(sum(n for g, _, n in WAVES if g == group) for group in range(3))
TILE_ROWS = 16
CHUNKS = (((0, 8),), ((0, 8),), ((0, 4), (4, 2), (6, 2)))
FAR_PIECES = tuple((cc, c, g) for cc in range(2) for c in range(len(CHUNKS[1 + cc])) for g in range(2))
NO_TILE = 3e38

FIRST_COL = (0, 4, 6)
LIST_AT = TILE_ROWS
TABLE = (TILE_ROWS + 8, BLOCK)


def remote(src, dst, send_sem, recv_sem, device):
    return pltpu.make_async_remote_copy(
        src_ref=src, dst_ref=dst, send_sem=send_sem, recv_sem=recv_sem,
        device_id=device, device_id_type=MESH,
    )


def scratch_list(tokens):
    dma = pltpu.SemaphoreType.DMA
    shapes = dict(
        mask=pltpu.VMEM((4 * TILE_ROWS, 8), I32),
        table_made=pltpu.VMEM(TABLE, I32),
        table=pltpu.SMEM(TABLE, I32),
        acts=pltpu.VMEM((tokens, TILE_ROWS * BLOCK), BF16),
        acts_t=pltpu.VMEM((TILE_ROWS, BLOCK, tokens), BF16),
        landed=pltpu.VMEM((32, 2, 2, 8, BLOCK), F32),
        in_sem=dma((7,)),
        pair_send=dma((4,)), pair_recv=dma((4,)),
        far_send=dma((len(FAR_PIECES),)), far_recv=dma((len(FAR_PIECES),)),
        fwd_send=dma((len(FAR_PIECES),)), fwd_recv=dma((len(FAR_PIECES),)),
    )
    for g, cols in enumerate(GROUP_COLS):
        n = GROUP_SLOTS[g]
        for c, (_, eighths) in enumerate(CHUNKS[g]):
            shapes[f"cots{g}_{c}"] = pltpu.VMEM((cols, eighths * tokens // 8, 2 * BLOCK), BF16)
        shapes[f"tiles{g}"] = pltpu.VMEM((n + 1, 8, BLOCK), F32)
        per_owner = (2, 2) if g == 0 else (2,)
        shapes[f"dense{g}"] = pltpu.VMEM((16, *per_owner, 8, BLOCK), F32)
        shapes[f"out_send{g}"] = dma((16,))
        shapes[f"out_recv{g}"] = dma((32,))
    for w, (_, _, n) in enumerate(WAVES):
        half = n // 2
        shapes[f"part{w}"] = pltpu.VMEM((2, 16, n, 8, BLOCK), F32)
        shapes[f"relay1_{w}"] = pltpu.VMEM((2, 2, 2, n, 8, BLOCK), F32)
        shapes[f"final1_{w}"] = pltpu.VMEM((2, 4, 2, n, 8, BLOCK), F32)
        shapes[f"relay2_{w}"] = pltpu.VMEM((2, 2, half, 8, BLOCK), F32)
        shapes[f"final2_{w}"] = pltpu.VMEM((2, 4, half, 8, BLOCK), F32)
        shapes[f"mid{w}"] = pltpu.VMEM((2, 4, n, 8, BLOCK), F32)
        shapes[f"last{w}"] = pltpu.VMEM((2, n, 8, BLOCK), F32)
        shapes[f"over{w}"] = pltpu.VMEM((n, 8, BLOCK), F32)
        shapes[f"ring_send{w}"] = dma((2, 2, 6))
        shapes[f"ring_recv{w}"] = dma((2, 2, 6))
        shapes[f"swap_send{w}"] = dma((1,))
        shapes[f"swap_recv{w}"] = dma((1,))
    return shapes


def make_table(m, round_ref, mask_ref, table_ref, rounds_ref):
    half = m // 2
    own = mask_ref[pl.ds(pl.multiple_of(m * TILE_ROWS, TILE_ROWS), TILE_ROWS), :]
    kept_all = jnp.where(own > 0, 1, 0)
    row_index = lax.broadcasted_iota(I32, (TILE_ROWS, 1), 0)
    slot_index = lax.broadcasted_iota(I32, (TILE_ROWS, BLOCK), 1)
    lane = lax.broadcasted_iota(I32, (TILE_ROWS, BLOCK), 1)
    before_rows = lax.broadcasted_iota(I32, (TILE_ROWS, TILE_ROWS), 1) < lax.broadcasted_iota(
        I32, (TILE_ROWS, TILE_ROWS), 0
    )
    place = jnp.zeros((TILE_ROWS, BLOCK), I32)
    lines = []
    for g, cols in enumerate(GROUP_COLS):
        n = GROUP_SLOTS[g]
        near, other = (
            [half_ * 4 + k for k in range(4)] if g == 0 else [(1 - half_) * 4 + k * 2 + g - 1 for k in range(2)]
            for half_ in range(2)
        )
        kept = [
            jnp.where(half == 0, kept_all[:, near[k] : near[k] + 1], kept_all[:, other[k] : other[k] + 1])
            for k in range(cols)
        ]
        per_row = functools.reduce(lambda p, q: p + q, kept)
        turned = jnp.sum(
            jnp.where(
                lax.broadcasted_iota(I32, (TILE_ROWS, TILE_ROWS), 0)
                == lax.broadcasted_iota(I32, (TILE_ROWS, TILE_ROWS), 1),
                per_row, 0,
            ),
            axis=0, keepdims=True,
        )
        seen = jnp.sum(jnp.where(before_rows, turned, 0), axis=1, keepdims=True) - round_ref[0] * n
        rows_line = jnp.zeros((1, BLOCK), I32)
        cols_line = jnp.zeros((1, BLOCK), I32)
        for k in range(cols):
            here = (kept[k] > 0) & (seen >= 0) & (seen < n)
            place = jnp.where(lane == FIRST_COL[g] + k, jnp.where(here, seen, n), place)
            chosen = jnp.where(here, seen, -1) == slot_index
            rows_line = rows_line + jnp.sum(jnp.where(chosen, row_index, 0), axis=0, keepdims=True)
            cols_line = cols_line + jnp.sum(jnp.where(chosen, k, 0), axis=0, keepdims=True)
            seen = seen + kept[k]
        lines += [rows_line, cols_line]

    counts = jnp.sum(jnp.where(mask_ref[...] > 0, 1, 0).reshape(4, TILE_ROWS, 8), axis=1)
    source = lax.broadcasted_iota(I32, (4, 8), 0)
    column = lax.broadcasted_iota(I32, (4, 8), 1)
    near = (source // 2) == (column // 4)
    even = lax.rem(column, 2) == 0
    needed = jnp.zeros((4, 1), I32)
    for g, inside in enumerate((near, ~near & even, ~near & ~even)):
        filled = jnp.sum(jnp.where(inside, counts, 0), axis=1, keepdims=True)
        rounds = sum(jnp.where(filled > n * GROUP_SLOTS[g], 1, 0) for n in range(TILE_ROWS * GROUP_COLS[g] // GROUP_SLOTS[g] + 1))
        needed = jnp.maximum(needed, rounds)
    rounds_ref[0] = jnp.max(needed)
    lines.append(jnp.zeros((2, BLOCK), I32))
    table_ref[pl.ds(0, TILE_ROWS)] = place
    table_ref[pl.ds(TILE_ROWS, 8)] = jnp.concatenate(lines, axis=0)


def kernel(*refs):
    refs = list(refs)
    names = list(scratch_list(8))
    r = dict(zip(names, refs[-len(names):]))
    round_ref, mask_hbm, acts_hbm, true_ref, sampled_ref, sums_ref, rounds_ref = refs[: -len(names)]
    table_ref = r["table"]

    dp = lax.axis_index("dp")
    m = lax.axis_index("mp")
    x, z, h = dp // 8, lax.rem(dp // 2, 4), lax.rem(dp, 2)
    l, core = m // 2, lax.rem(m, 2)

    def device_at(x, z, h, m):
        return (x * 8 + z * 2 + h, m)

    pair = device_at(x, z, h, l * 2 + 1 - core)
    far = device_at(x, z, h, (1 - l) * 2 + core)
    along_x = [device_at(lax.rem(x + d, 4), z, h, m) for d in (1, 3)]
    along_z = [device_at(x, lax.rem(z + d, 4), h, m) for d in (1, 3)]
    across_h = device_at(x, z, 1 - h, m)

    acts_in = pltpu.make_async_copy(acts_hbm, r["acts"], r["in_sem"].at[0])
    mask_in = pltpu.make_async_copy(mask_hbm, r["mask"], r["in_sem"].at[5])
    mask_in.start()
    acts_in.start()

    barrier = pltpu.get_barrier_semaphore()
    for other in (pair, far, *along_x, *along_z, across_h):
        pl.semaphore_signal(barrier, inc=1, device_id=other, device_id_type=MESH)

    def greet(sender, carry):
        @pl.when(jnp.logical_not(jnp.logical_and(sender == dp, m == x)))
        def _():
            pl.semaphore_signal(barrier, inc=1, device_id=(sender, x), device_id_type=MESH)
        return carry

    lax.fori_loop(0, 32, greet, 0)
    pl.semaphore_wait(barrier, jnp.where(m == x, 38, 39))

    eighth = true_ref.shape[0] // 8

    def own(cc, g, first=0, count=8):
        return (true_ref, sampled_ref)[g].at[pl.ds(first * eighth, count * eighth), lanes(cc)]

    def lanes(g):
        return pl.ds(g * BLOCK, BLOCK)

    def far_place(cc, c, g):
        return r[f"cots{1 + cc}_{c}"].at[core, :, lanes(g)]

    inputs, pairs, fars, fwds, started = [], [], [], {}, []
    for i, (cc, c, g) in enumerate(FAR_PIECES):
        piece = own(cc, g, *CHUNKS[1 + cc][c])
        fars.append(remote(piece, far_place(cc, c, g), r["far_send"].at[i], r["far_recv"].at[i], far))
    for i, (cc, g) in enumerate((cc, g) for cc in range(2) for g in range(2)):
        near_place = r["cots0_0"].at[core * 2 + cc, :, lanes(g)]
        pairs.append(remote(own(cc, g), near_place, r["pair_send"].at[i], r["pair_recv"].at[i], pair))
        inputs.append(pltpu.make_async_copy(own(cc, g), near_place, r["in_sem"].at[1 + i]))
    for copies in (fars, pairs, inputs):
        for copy in copies:
            copy.start()
    mask_in.wait()
    make_table(m, round_ref, r["mask"], r["table_made"], rounds_ref)
    table_in = pltpu.make_async_copy(r["table_made"], r["table"], r["in_sem"].at[6])
    table_in.start()
    acts_in.wait()

    def transpose(row, carry):
        r["acts_t"][row] = r["acts"][:, pl.ds(pl.multiple_of(row * BLOCK, BLOCK), BLOCK)].T
        return carry

    lax.fori_loop(0, TILE_ROWS, transpose, 0)

    def products(w, c=0):
        group, first, n = WAVES[w]
        cots, part = r[f"cots{group}_{c}"], r[f"part{w}"]
        start, count = CHUNKS[group][c]

        def one(i, carry):
            for u in range(2):
                s = 2 * i + u
                row = table_ref[LIST_AT + 2 * group, first + s]
                col = table_ref[LIST_AT + 2 * group + 1, first + s]
                strip = r["acts_t"][row][:, start * eighth : (start + count) * eighth]
                tile = jnp.dot(strip, cots[col], preferred_element_type=F32)
                for g in range(2):
                    term = tile[:, g * BLOCK : (g + 1) * BLOCK].reshape(16, 8, BLOCK)
                    part[g, :, s] = term if c == 0 else part[g, :, s] + term
            return carry

        lax.fori_loop(0, n // 2, one, 0)

    def ring_open(send, recv, pos, neighbours, chunk, relay, final):
        up, down = neighbours
        nxt, opposite, prv = (lax.rem(pos + d, 4) for d in (1, 2, 3))
        copies = [
            remote(chunk(opposite, 0), relay.at[0], send.at[0], recv.at[0], up),
            remote(chunk(opposite, 1), relay.at[1], send.at[1], recv.at[1], down),
            remote(chunk(nxt, 1), final.at[0], send.at[2], recv.at[2], up),
            remote(chunk(prv, 0), final.at[1], send.at[3], recv.at[3], down),
            remote(relay.at[0], final.at[2], send.at[4], recv.at[4], up),
            remote(relay.at[1], final.at[3], send.at[5], recv.at[5], down),
        ]
        for copy in copies[:4]:
            copy.start()
        started.extend(copies)
        return copies

    def ring_turn(copies, pos, chunk, relay, add):
        for i, d in enumerate((1, 3)):
            copies[i].wait_recv()
            add(relay.at[i], (relay.at[i], chunk(lax.rem(pos + d, 4), i)))
            copies[4 + i].start()

    def ring_close(copies, pos, chunk, final, add, result):
        for copy in copies[2:]:
            copy.wait_recv()
        add(result(0), (chunk(pos, 0), final.at[1], final.at[2]))
        add(result(1), (chunk(pos, 1), final.at[0], final.at[3]))

    def add_big(dst, srcs):
        for i in range(2):
            total = srcs[0][i] + srcs[1][i]
            for src in srcs[2:]:
                total = total + src[i]
            dst[i] = total

    def add_small(dst, srcs):
        total = srcs[0][...] + srcs[1][...]
        for src in srcs[2:]:
            total = total + src[...]
        dst[...] = total

    streams = ((x, along_x, z, along_z), (z, along_z, x, along_x))
    first_ring, second_ring, swaps = {}, {}, {}

    def chunk1(w, s):
        return lambda p, half: r[f"part{w}"].at[s, pl.ds(p * 4 + half * 2, 2)]

    def chunk2(w, s):
        half_n = WAVES[w][2] // 2
        return lambda p, half: r[f"mid{w}"].at[s, p, pl.ds(half * half_n, half_n)]

    def open_first(w):
        for s, (pos, near, _, _) in enumerate(streams):
            first_ring[w, s] = ring_open(
                r[f"ring_send{w}"].at[s, 0], r[f"ring_recv{w}"].at[s, 0], pos, near, chunk1(w, s),
                r[f"relay1_{w}"].at[s], r[f"final1_{w}"].at[s],
            )

    def turn_first(w):
        for s, (pos, _, _, _) in enumerate(streams):
            ring_turn(first_ring[w, s], pos, chunk1(w, s), r[f"relay1_{w}"].at[s], add_big)

    def close_first(w):
        for s, (pos, _, pos2, near2) in enumerate(streams):
            ring_close(
                first_ring[w, s], pos, chunk1(w, s), r[f"final1_{w}"].at[s], add_big,
                lambda half: r[f"mid{w}"].at[s, pl.ds(half * 2, 2)],
            )
            second_ring[w, s] = ring_open(
                r[f"ring_send{w}"].at[s, 1], r[f"ring_recv{w}"].at[s, 1], pos2, near2, chunk2(w, s),
                r[f"relay2_{w}"].at[s], r[f"final2_{w}"].at[s],
            )

    def turn_second(w):
        for s, (_, _, pos2, _) in enumerate(streams):
            ring_turn(second_ring[w, s], pos2, chunk2(w, s), r[f"relay2_{w}"].at[s], add_small)

    def close_second(w):
        half_n = WAVES[w][2] // 2
        for s, (_, _, pos2, _) in enumerate(streams):
            ring_close(
                second_ring[w, s], pos2, chunk2(w, s), r[f"final2_{w}"].at[s], add_small,
                lambda half: r[f"last{w}"].at[s, pl.ds(half * half_n, half_n)],
            )
        swaps[w] = remote(
            r[f"last{w}"].at[1 - h], r[f"over{w}"], r[f"swap_send{w}"].at[0], r[f"swap_recv{w}"].at[0], across_h
        )
        swaps[w].start()
        started.append(swaps[w])

    def owner(g, t):
        return m * 8 + t // 2, (l if g == 0 else 1 - l) * 2 + lax.rem(t, 2)

    def itself(g, t):
        return jnp.logical_and(owner(g, t)[0] == dp, owner(g, t)[1] == m)

    def spot(g):
        return r["landed"].at[dp] if g == 0 else r["landed"].at[dp, g - 1]

    def outgoing(g, t):
        return remote(r[f"dense{g}"].at[t], spot(g), r[f"out_send{g}"].at[t], r[f"out_recv{g}"].at[dp], owner(g, t))

    def deliver(g):
        tiles, dense = r[f"tiles{g}"], r[f"dense{g}"]
        for w, (group, first, n) in enumerate(WAVES):
            if group == g:
                swaps[w].wait_recv()
                tiles[pl.ds(first, n)] = r[f"last{w}"][h] + r[f"over{w}"][...]
        tiles[GROUP_SLOTS[g]] = jnp.full((8, BLOCK), NO_TILE, F32)

        def one(t, carry):
            core_to = lax.rem(t, 2)
            for lo in range(2):
                row = (t // 2) * 2 + lo
                if g == 0:
                    for cc in range(2):
                        dense[t, cc, lo] = tiles[table_ref[row, core_to * 2 + cc]]
                else:
                    dense[t, lo] = tiles[table_ref[row, FIRST_COL[g] + core_to]]

            @pl.when(itself(g, t))
            def _():
                pltpu.make_async_copy(dense.at[t], spot(g), r[f"out_recv{g}"].at[dp]).start()

            @pl.when(jnp.logical_not(itself(g, t)))
            def _():
                outgoing(g, t).start()

            return carry

        lax.fori_loop(0, 16, one, 0)

    def drain(g):
        def one(t, carry):
            @pl.when(jnp.logical_not(itself(g, t)))
            def _():
                outgoing(g, t).wait_send()

            return carry

        lax.fori_loop(0, 16, one, 0)

    def forward(cc, c=0):
        for i, piece in enumerate(FAR_PIECES):
            if piece[:2] == (cc, c):
                fars[i].wait_recv()
                place = far_place(*piece)
                fwds[piece] = remote(place, place, r["fwd_send"].at[i], r["fwd_recv"].at[i], pair)
                fwds[piece].start()

    def forwarded(cc, c=0):
        for piece in FAR_PIECES:
            if piece[:2] == (cc, c):
                fwds[piece].wait_recv()

    table_in.wait()
    for copy in inputs:
        copy.wait()
    for copy in pairs:
        copy.wait_recv()
    products(0)
    open_first(0)
    products(1)
    open_first(1)
    turn_first(0)
    forward(0)
    turn_first(1)
    forwarded(0)
    products(2)
    open_first(2)
    close_first(0)
    forward(1, 0)
    close_first(1)
    forwarded(1, 0)
    products(3, 0)
    forward(1, 1)
    forwarded(1, 1)
    products(3, 1)
    turn_first(2)
    forward(1, 2)
    forwarded(1, 2)
    products(3, 2)
    open_first(3)
    turn_second(0)
    turn_second(1)
    close_second(0)
    close_second(1)
    close_first(2)
    turn_first(3)
    turn_second(2)
    close_second(2)
    close_first(3)
    turn_second(3)
    deliver(0)
    deliver(1)
    close_second(3)
    deliver(2)

    def arrived(g):
        def one(i, carry):
            place = r["landed"].at[i] if g == 0 else r["landed"].at[i, g - 1]
            pltpu.make_async_copy(place, place, r[f"out_recv{g}"].at[i]).wait()
            return carry

        lax.fori_loop(0, 32, one, 0)

    @pl.when(m // 2 == x // 2)
    def _():
        arrived(0)

    @pl.when(m // 2 != x // 2)
    def _():
        arrived(1)
        arrived(2)

    def finish(strip, carry):
        from_true = strip * 2
        from_sampled = (lax.rem(strip, 4) * 4 + strip // 4) * 2 + 1
        for cc in range(2):
            for lo in range(2):
                at = (pl.ds(pl.multiple_of(lo * BLOCK + strip * 8, 8), 8), pl.ds(cc * BLOCK, BLOCK))
                sums_ref[(0, *at)] = r["landed"][from_true, cc, lo]
                sums_ref[(1, *at)] = r["landed"][from_sampled, cc, lo]
        return carry

    lax.fori_loop(0, 16, finish, 0)

    for copy in (*fars, *pairs, *fwds.values(), *started):
        copy.wait_send()
    for g in range(3):
        drain(g)


def round_step(*args):
    smem = pl.BlockSpec(memory_space=pltpu.SMEM)
    hbm = pl.BlockSpec(memory_space=pl.ANY)
    return pl.pallas_call(
        kernel,
        out_shape=(jax.ShapeDtypeStruct((2, 2 * BLOCK, 2 * BLOCK), F32), jax.ShapeDtypeStruct((1,), I32)),
        in_specs=[smem, hbm, hbm, hbm, hbm],
        out_specs=(pl.BlockSpec(memory_space=pltpu.VMEM), smem),
        scratch_shapes=list(scratch_list(args[2].shape[0]).values()),
        compiler_params=pltpu.CompilerParams(
            collective_id=0, has_side_effects=True, vmem_limit_bytes=60 << 20
        ),
        name="round_step",
    )(*args)


def on_device(activations, cot_true, cot_sampled, tile_mask, moment, curvature):
    tokens_all = activations.shape[0] * lax.axis_size("dp")

    def one_round(round_):
        return round_step(round_.reshape(1), tile_mask, activations, cot_true, cot_sampled)

    sums, rounds = one_round(jnp.int32(0))
    def again(state):
        found, _ = one_round(state[0])
        return state[0] + 1, jnp.where(found < NO_TILE / 2, found, state[1])

    _, sums = lax.while_loop(lambda state: state[0] < rounds[0], again, (jnp.int32(1), sums))
    kept = sums[0] < NO_TILE / 2
    grads = sums * (1.0 / tokens_all)
    moment_new = BETA_ONE * moment + (1.0 - BETA_ONE) * grads[0]
    hessian = tokens_all * grads[1] * grads[1]
    curvature_next = BETA_TWO * curvature + (1.0 - BETA_TWO) * hessian
    update = jnp.clip(moment_new / (GAMMA_CLIP * curvature_next), -1.0, 1.0)
    return jnp.where(kept, update, 0.0), jnp.where(kept, curvature_next, 0.0)


def solution(mesh):
    return jax.shard_map(
        on_device,
        mesh=mesh,
        in_specs=(P("dp", "mp"), P("dp", "mp"), P("dp", "mp"), P(), P("dp", "mp"), P("dp", "mp")),
        out_specs=(P("dp", "mp"), P("dp", "mp")),
        check_vma=False,
    )
```

```python
import functools

import jax
import jax.numpy as jnp
from jax import lax
from jax.experimental import pallas as pl
from jax.experimental.pallas import tpu as pltpu
from jax.sharding import PartitionSpec as P

D = 8192
BLOCK = 128
BETA_ONE = 0.965
BETA_TWO = 0.99
GAMMA_CLIP = 0.01
MESH = pl.DeviceIdType.MESH
F32, BF16, I32 = jnp.float32, jnp.bfloat16, jnp.int32

GROUP_COLS = (4, 2, 2)
WAVES = ((0, 0, 14), (0, 14, 12), (1, 0, 16), (2, 0, 16))
GROUP_SLOTS = tuple(sum(n for g, _, n in WAVES if g == group) for group in range(3))
TILE_ROWS = 16
CHUNKS = (((0, 8),), ((0, 8),), ((0, 4), (4, 2), (6, 2)))
FAR_PIECES = tuple((cc, c, g) for cc in range(2) for c in range(len(CHUNKS[1 + cc])) for g in range(2))
NO_TILE = 3e38

FIRST_COL = (0, 4, 6)
LIST_AT = TILE_ROWS
TABLE = (TILE_ROWS + 8, BLOCK)


def remote(src, dst, send_sem, recv_sem, device):
    return pltpu.make_async_remote_copy(
        src_ref=src, dst_ref=dst, send_sem=send_sem, recv_sem=recv_sem,
        device_id=device, device_id_type=MESH,
    )


def scratch_list(tokens):
    dma = pltpu.SemaphoreType.DMA
    shapes = dict(
        mask=pltpu.VMEM((4 * TILE_ROWS, 8), I32),
        table_made=pltpu.VMEM(TABLE, I32),
        table=pltpu.SMEM(TABLE, I32),
        acts=pltpu.VMEM((tokens, TILE_ROWS * BLOCK), BF16),
        acts_t=pltpu.VMEM((TILE_ROWS, BLOCK, tokens), BF16),
        landed=pltpu.VMEM((32, 2, 2, 8, BLOCK), F32),
        in_sem=dma((7,)),
        pair_send=dma((4,)), pair_recv=dma((4,)),
        far_send=dma((len(FAR_PIECES),)), far_recv=dma((len(FAR_PIECES),)),
        fwd_send=dma((len(FAR_PIECES),)), fwd_recv=dma((len(FAR_PIECES),)),
    )
    for g, cols in enumerate(GROUP_COLS):
        n = GROUP_SLOTS[g]
        for c, (_, eighths) in enumerate(CHUNKS[g]):
            shapes[f"cots{g}_{c}"] = pltpu.VMEM((cols, eighths * tokens // 8, 2 * BLOCK), BF16)
        shapes[f"tiles{g}"] = pltpu.VMEM((n + 1, 8, BLOCK), F32)
        per_owner = (2, 2) if g == 0 else (2,)
        shapes[f"dense{g}"] = pltpu.VMEM((16, *per_owner, 8, BLOCK), F32)
        shapes[f"out_send{g}"] = dma((16,))
        shapes[f"out_recv{g}"] = dma((32,))
    for w, (_, _, n) in enumerate(WAVES):
        half = n // 2
        shapes[f"part{w}"] = pltpu.VMEM((2, 16, n, 8, BLOCK), F32)
        shapes[f"relay1_{w}"] = pltpu.VMEM((2, 2, 2, n, 8, BLOCK), F32)
        shapes[f"final1_{w}"] = pltpu.VMEM((2, 4, 2, n, 8, BLOCK), F32)
        shapes[f"relay2_{w}"] = pltpu.VMEM((2, 2, half, 8, BLOCK), F32)
        shapes[f"final2_{w}"] = pltpu.VMEM((2, 4, half, 8, BLOCK), F32)
        shapes[f"mid{w}"] = pltpu.VMEM((2, 4, n, 8, BLOCK), F32)
        shapes[f"last{w}"] = pltpu.VMEM((2, n, 8, BLOCK), F32)
        shapes[f"over{w}"] = pltpu.VMEM((n, 8, BLOCK), F32)
        shapes[f"ring_send{w}"] = dma((2, 2, 6))
        shapes[f"ring_recv{w}"] = dma((2, 2, 6))
        shapes[f"swap_send{w}"] = dma((1,))
        shapes[f"swap_recv{w}"] = dma((1,))
    return shapes


def make_table(m, round_ref, mask_ref, table_ref, rounds_ref):
    half = m // 2
    own = mask_ref[pl.ds(pl.multiple_of(m * TILE_ROWS, TILE_ROWS), TILE_ROWS), :]
    kept_all = jnp.where(own > 0, 1, 0)
    row_index = lax.broadcasted_iota(I32, (TILE_ROWS, 1), 0)
    slot_index = lax.broadcasted_iota(I32, (TILE_ROWS, BLOCK), 1)
    lane = lax.broadcasted_iota(I32, (TILE_ROWS, BLOCK), 1)
    before_rows = lax.broadcasted_iota(I32, (TILE_ROWS, TILE_ROWS), 1) < lax.broadcasted_iota(
        I32, (TILE_ROWS, TILE_ROWS), 0
    )
    place = jnp.zeros((TILE_ROWS, BLOCK), I32)
    lines = []
    for g, cols in enumerate(GROUP_COLS):
        n = GROUP_SLOTS[g]
        near, other = (
            [half_ * 4 + k for k in range(4)] if g == 0 else [(1 - half_) * 4 + k * 2 + g - 1 for k in range(2)]
            for half_ in range(2)
        )
        kept = [
            jnp.where(half == 0, kept_all[:, near[k] : near[k] + 1], kept_all[:, other[k] : other[k] + 1])
            for k in range(cols)
        ]
        per_row = functools.reduce(lambda p, q: p + q, kept)
        turned = jnp.sum(
            jnp.where(
                lax.broadcasted_iota(I32, (TILE_ROWS, TILE_ROWS), 0)
                == lax.broadcasted_iota(I32, (TILE_ROWS, TILE_ROWS), 1),
                per_row, 0,
            ),
            axis=0, keepdims=True,
        )
        seen = jnp.sum(jnp.where(before_rows, turned, 0), axis=1, keepdims=True) - round_ref[0] * n
        rows_line = jnp.zeros((1, BLOCK), I32)
        cols_line = jnp.zeros((1, BLOCK), I32)
        for k in range(cols):
            here = (kept[k] > 0) & (seen >= 0) & (seen < n)
            place = jnp.where(lane == FIRST_COL[g] + k, jnp.where(here, seen, n), place)
            chosen = jnp.where(here, seen, -1) == slot_index
            rows_line = rows_line + jnp.sum(jnp.where(chosen, row_index, 0), axis=0, keepdims=True)
            cols_line = cols_line + jnp.sum(jnp.where(chosen, k, 0), axis=0, keepdims=True)
            seen = seen + kept[k]
        lines += [rows_line, cols_line]

    counts = jnp.sum(jnp.where(mask_ref[...] > 0, 1, 0).reshape(4, TILE_ROWS, 8), axis=1)
    source = lax.broadcasted_iota(I32, (4, 8), 0)
    column = lax.broadcasted_iota(I32, (4, 8), 1)
    near = (source // 2) == (column // 4)
    even = lax.rem(column, 2) == 0
    needed = jnp.zeros((4, 1), I32)
    for g, inside in enumerate((near, ~near & even, ~near & ~even)):
        filled = jnp.sum(jnp.where(inside, counts, 0), axis=1, keepdims=True)
        rounds = sum(jnp.where(filled > n * GROUP_SLOTS[g], 1, 0) for n in range(TILE_ROWS * GROUP_COLS[g] // GROUP_SLOTS[g] + 1))
        needed = jnp.maximum(needed, rounds)
    rounds_ref[0] = jnp.max(needed)
    lines.append(jnp.zeros((2, BLOCK), I32))
    table_ref[pl.ds(0, TILE_ROWS)] = place
    table_ref[pl.ds(TILE_ROWS, 8)] = jnp.concatenate(lines, axis=0)


def kernel(*refs):
    refs = list(refs)
    names = list(scratch_list(8))
    r = dict(zip(names, refs[-len(names):]))
    round_ref, mask_hbm, acts_hbm, true_ref, sampled_ref, sums_ref, rounds_ref = refs[: -len(names)]
    table_ref = r["table"]

    dp = lax.axis_index("dp")
    m = lax.axis_index("mp")
    x, z, h = dp // 8, lax.rem(dp // 2, 4), lax.rem(dp, 2)
    l, core = m // 2, lax.rem(m, 2)

    def device_at(x, z, h, m):
        return (x * 8 + z * 2 + h, m)

    pair = device_at(x, z, h, l * 2 + 1 - core)
    far = device_at(x, z, h, (1 - l) * 2 + core)
    along_x = [device_at(lax.rem(x + d, 4), z, h, m) for d in (1, 3)]
    along_z = [device_at(x, lax.rem(z + d, 4), h, m) for d in (1, 3)]
    across_h = device_at(x, z, 1 - h, m)

    acts_in = pltpu.make_async_copy(acts_hbm, r["acts"], r["in_sem"].at[0])
    mask_in = pltpu.make_async_copy(mask_hbm, r["mask"], r["in_sem"].at[5])
    mask_in.start()
    acts_in.start()

    barrier = pltpu.get_barrier_semaphore()
    for other in (pair, far, *along_x, *along_z, across_h):
        pl.semaphore_signal(barrier, inc=1, device_id=other, device_id_type=MESH)

    pl.semaphore_wait(barrier, 7)

    eighth = true_ref.shape[0] // 8

    def own(cc, g, first=0, count=8):
        return (true_ref, sampled_ref)[g].at[pl.ds(first * eighth, count * eighth), lanes(cc)]

    def lanes(g):
        return pl.ds(g * BLOCK, BLOCK)

    def far_place(cc, c, g):
        return r[f"cots{1 + cc}_{c}"].at[core, :, lanes(g)]

    inputs, pairs, fars, fwds, started = [], [], [], {}, []
    for i, (cc, c, g) in enumerate(FAR_PIECES):
        piece = own(cc, g, *CHUNKS[1 + cc][c])
        fars.append(remote(piece, far_place(cc, c, g), r["far_send"].at[i], r["far_recv"].at[i], far))
    for i, (cc, g) in enumerate((cc, g) for cc in range(2) for g in range(2)):
        near_place = r["cots0_0"].at[core * 2 + cc, :, lanes(g)]
        pairs.append(remote(own(cc, g), near_place, r["pair_send"].at[i], r["pair_recv"].at[i], pair))
        inputs.append(pltpu.make_async_copy(own(cc, g), near_place, r["in_sem"].at[1 + i]))
    for copies in (fars, pairs, inputs):
        for copy in copies:
            copy.start()
    mask_in.wait()
    make_table(m, round_ref, r["mask"], r["table_made"], rounds_ref)
    table_in = pltpu.make_async_copy(r["table_made"], r["table"], r["in_sem"].at[6])
    table_in.start()
    acts_in.wait()

    def transpose(row, carry):
        r["acts_t"][row] = r["acts"][:, pl.ds(pl.multiple_of(row * BLOCK, BLOCK), BLOCK)].T
        return carry

    lax.fori_loop(0, TILE_ROWS, transpose, 0)

    def products(w, c=0):
        group, first, n = WAVES[w]
        cots, part = r[f"cots{group}_{c}"], r[f"part{w}"]
        start, count = CHUNKS[group][c]

        def one(i, carry):
            for u in range(2):
                s = 2 * i + u
                row = table_ref[LIST_AT + 2 * group, first + s]
                col = table_ref[LIST_AT + 2 * group + 1, first + s]
                strip = r["acts_t"][row][:, start * eighth : (start + count) * eighth]
                tile = jnp.dot(strip, cots[col], preferred_element_type=F32)
                for g in range(2):
                    term = tile[:, g * BLOCK : (g + 1) * BLOCK].reshape(16, 8, BLOCK)
                    part[g, :, s] = term if c == 0 else part[g, :, s] + term
            return carry

        lax.fori_loop(0, n // 2, one, 0)

    def ring_open(send, recv, pos, neighbours, chunk, relay, final):
        up, down = neighbours
        nxt, opposite, prv = (lax.rem(pos + d, 4) for d in (1, 2, 3))
        copies = [
            remote(chunk(opposite, 0), relay.at[0], send.at[0], recv.at[0], up),
            remote(chunk(opposite, 1), relay.at[1], send.at[1], recv.at[1], down),
            remote(chunk(nxt, 1), final.at[0], send.at[2], recv.at[2], up),
            remote(chunk(prv, 0), final.at[1], send.at[3], recv.at[3], down),
            remote(relay.at[0], final.at[2], send.at[4], recv.at[4], up),
            remote(relay.at[1], final.at[3], send.at[5], recv.at[5], down),
        ]
        for copy in copies[:4]:
            copy.start()
        started.extend(copies)
        return copies

    def ring_turn(copies, pos, chunk, relay, add):
        for i, d in enumerate((1, 3)):
            copies[i].wait_recv()
            add(relay.at[i], (relay.at[i], chunk(lax.rem(pos + d, 4), i)))
            copies[4 + i].start()

    def ring_close(copies, pos, chunk, final, add, result):
        for copy in copies[2:]:
            copy.wait_recv()
        add(result(0), (chunk(pos, 0), final.at[1], final.at[2]))
        add(result(1), (chunk(pos, 1), final.at[0], final.at[3]))

    def add_big(dst, srcs):
        for i in range(2):
            total = srcs[0][i] + srcs[1][i]
            for src in srcs[2:]:
                total = total + src[i]
            dst[i] = total

    def add_small(dst, srcs):
        total = srcs[0][...] + srcs[1][...]
        for src in srcs[2:]:
            total = total + src[...]
        dst[...] = total

    streams = ((x, along_x, z, along_z), (z, along_z, x, along_x))
    first_ring, second_ring, swaps = {}, {}, {}

    def chunk1(w, s):
        return lambda p, half: r[f"part{w}"].at[s, pl.ds(p * 4 + half * 2, 2)]

    def chunk2(w, s):
        half_n = WAVES[w][2] // 2
        return lambda p, half: r[f"mid{w}"].at[s, p, pl.ds(half * half_n, half_n)]

    def open_first(w):
        for s, (pos, near, _, _) in enumerate(streams):
            first_ring[w, s] = ring_open(
                r[f"ring_send{w}"].at[s, 0], r[f"ring_recv{w}"].at[s, 0], pos, near, chunk1(w, s),
                r[f"relay1_{w}"].at[s], r[f"final1_{w}"].at[s],
            )

    def turn_first(w):
        for s, (pos, _, _, _) in enumerate(streams):
            ring_turn(first_ring[w, s], pos, chunk1(w, s), r[f"relay1_{w}"].at[s], add_big)

    def close_first(w):
        for s, (pos, _, pos2, near2) in enumerate(streams):
            ring_close(
                first_ring[w, s], pos, chunk1(w, s), r[f"final1_{w}"].at[s], add_big,
                lambda half: r[f"mid{w}"].at[s, pl.ds(half * 2, 2)],
            )
            second_ring[w, s] = ring_open(
                r[f"ring_send{w}"].at[s, 1], r[f"ring_recv{w}"].at[s, 1], pos2, near2, chunk2(w, s),
                r[f"relay2_{w}"].at[s], r[f"final2_{w}"].at[s],
            )

    def turn_second(w):
        for s, (_, _, pos2, _) in enumerate(streams):
            ring_turn(second_ring[w, s], pos2, chunk2(w, s), r[f"relay2_{w}"].at[s], add_small)

    def close_second(w):
        half_n = WAVES[w][2] // 2
        for s, (_, _, pos2, _) in enumerate(streams):
            ring_close(
                second_ring[w, s], pos2, chunk2(w, s), r[f"final2_{w}"].at[s], add_small,
                lambda half: r[f"last{w}"].at[s, pl.ds(half * half_n, half_n)],
            )
        swaps[w] = remote(
            r[f"last{w}"].at[1 - h], r[f"over{w}"], r[f"swap_send{w}"].at[0], r[f"swap_recv{w}"].at[0], across_h
        )
        swaps[w].start()
        started.append(swaps[w])

    def owner(g, t):
        return m * 8 + t // 2, (l if g == 0 else 1 - l) * 2 + lax.rem(t, 2)

    def itself(g, t):
        return jnp.logical_and(owner(g, t)[0] == dp, owner(g, t)[1] == m)

    def spot(g):
        return r["landed"].at[dp] if g == 0 else r["landed"].at[dp, g - 1]

    def outgoing(g, t):
        return remote(r[f"dense{g}"].at[t], spot(g), r[f"out_send{g}"].at[t], r[f"out_recv{g}"].at[dp], owner(g, t))

    def deliver(g):
        tiles, dense = r[f"tiles{g}"], r[f"dense{g}"]
        for w, (group, first, n) in enumerate(WAVES):
            if group == g:
                swaps[w].wait_recv()
                tiles[pl.ds(first, n)] = r[f"last{w}"][h] + r[f"over{w}"][...]
        tiles[GROUP_SLOTS[g]] = jnp.full((8, BLOCK), NO_TILE, F32)

        def one(t, carry):
            core_to = lax.rem(t, 2)
            for lo in range(2):
                row = (t // 2) * 2 + lo
                if g == 0:
                    for cc in range(2):
                        dense[t, cc, lo] = tiles[table_ref[row, core_to * 2 + cc]]
                else:
                    dense[t, lo] = tiles[table_ref[row, FIRST_COL[g] + core_to]]

            @pl.when(itself(g, t))
            def _():
                pltpu.make_async_copy(dense.at[t], spot(g), r[f"out_recv{g}"].at[dp]).start()

            @pl.when(jnp.logical_not(itself(g, t)))
            def _():
                outgoing(g, t).start()

            return carry

        lax.fori_loop(0, 16, one, 0)

    def drain(g):
        def one(t, carry):
            @pl.when(jnp.logical_not(itself(g, t)))
            def _():
                outgoing(g, t).wait_send()

            return carry

        lax.fori_loop(0, 16, one, 0)

    def forward(cc, c=0):
        for i, piece in enumerate(FAR_PIECES):
            if piece[:2] == (cc, c):
                fars[i].wait_recv()
                place = far_place(*piece)
                fwds[piece] = remote(place, place, r["fwd_send"].at[i], r["fwd_recv"].at[i], pair)
                fwds[piece].start()

    def forwarded(cc, c=0):
        for piece in FAR_PIECES:
            if piece[:2] == (cc, c):
                fwds[piece].wait_recv()

    table_in.wait()
    for copy in inputs:
        copy.wait()
    for copy in pairs:
        copy.wait_recv()
    products(0)
    open_first(0)
    products(1)
    open_first(1)
    turn_first(0)
    forward(0)
    turn_first(1)
    forwarded(0)
    products(2)
    open_first(2)
    close_first(0)
    forward(1, 0)
    close_first(1)
    forwarded(1, 0)
    products(3, 0)
    forward(1, 1)
    forwarded(1, 1)
    products(3, 1)
    turn_first(2)
    forward(1, 2)
    forwarded(1, 2)
    products(3, 2)
    open_first(3)
    turn_second(0)
    turn_second(1)
    close_second(0)
    close_second(1)
    close_first(2)
    turn_first(3)
    turn_second(2)
    close_second(2)
    close_first(3)
    turn_second(3)
    deliver(0)
    deliver(1)
    close_second(3)
    deliver(2)

    def arrived(g):
        def one(i, carry):
            place = r["landed"].at[i] if g == 0 else r["landed"].at[i, g - 1]
            pltpu.make_async_copy(place, place, r[f"out_recv{g}"].at[i]).wait()
            return carry

        lax.fori_loop(0, 32, one, 0)

    @pl.when(m // 2 == x // 2)
    def _():
        arrived(0)

    @pl.when(m // 2 != x // 2)
    def _():
        arrived(1)
        arrived(2)

    def finish(strip, carry):
        from_true = strip * 2
        from_sampled = (lax.rem(strip, 4) * 4 + strip // 4) * 2 + 1
        for cc in range(2):
            for lo in range(2):
                at = (pl.ds(pl.multiple_of(lo * BLOCK + strip * 8, 8), 8), pl.ds(cc * BLOCK, BLOCK))
                sums_ref[(0, *at)] = r["landed"][from_true, cc, lo]
                sums_ref[(1, *at)] = r["landed"][from_sampled, cc, lo]
        return carry

    lax.fori_loop(0, 16, finish, 0)

    for copy in (*fars, *pairs, *fwds.values(), *started):
        copy.wait_send()
    for g in range(3):
        drain(g)


def round_step(*args):
    smem = pl.BlockSpec(memory_space=pltpu.SMEM)
    hbm = pl.BlockSpec(memory_space=pl.ANY)
    return pl.pallas_call(
        kernel,
        out_shape=(jax.ShapeDtypeStruct((2, 2 * BLOCK, 2 * BLOCK), F32), jax.ShapeDtypeStruct((1,), I32)),
        in_specs=[smem, hbm, hbm, hbm, hbm],
        out_specs=(pl.BlockSpec(memory_space=pltpu.VMEM), smem),
        scratch_shapes=list(scratch_list(args[2].shape[0]).values()),
        compiler_params=pltpu.CompilerParams(
            collective_id=0, has_side_effects=True, vmem_limit_bytes=60 << 20
        ),
        name="round_step",
    )(*args)


def on_device(activations, cot_true, cot_sampled, tile_mask, moment, curvature):
    tokens_all = activations.shape[0] * lax.axis_size("dp")

    def one_round(round_):
        return round_step(round_.reshape(1), tile_mask, activations, cot_true, cot_sampled)

    sums, rounds = one_round(jnp.int32(0))
    def again(state):
        found, _ = one_round(state[0])
        return state[0] + 1, jnp.where(found < NO_TILE / 2, found, state[1])

    _, sums = lax.while_loop(lambda state: state[0] < rounds[0], again, (jnp.int32(1), sums))
    kept = sums[0] < NO_TILE / 2
    grads = sums * (1.0 / tokens_all)
    moment_new = BETA_ONE * moment + (1.0 - BETA_ONE) * grads[0]
    hessian = tokens_all * grads[1] * grads[1]
    curvature_next = BETA_TWO * curvature + (1.0 - BETA_TWO) * hessian
    update = jnp.clip(moment_new / (GAMMA_CLIP * curvature_next), -1.0, 1.0)
    return jnp.where(kept, update, 0.0), jnp.where(kept, curvature_next, 0.0)


def solution(mesh):
    return jax.shard_map(
        on_device,
        mesh=mesh,
        in_specs=(P("dp", "mp"), P("dp", "mp"), P("dp", "mp"), P(), P("dp", "mp"), P("dp", "mp")),
        out_specs=(P("dp", "mp"), P("dp", "mp")),
        check_vma=False,
    )
```
